32 devices in a mesh: pipe: 1, expert: 32 (over z, y, x, core).
Axes of the slice: x: 2, y: 2, z: 4, core: 2. Of those that a mesh axis runs over, the one named last changes fastest.
Arguments:
- inputs: bfloat16 [1, 2, 2048, 2048], P('pipe', None, 'expert'), may hold values from -6 to 6
- grads_out: bfloat16 [1, 2, 2048, 2048], P('pipe', None, 'expert'), may hold values from -6 to 6
- expert_ids: int32 [1, 2, 2048, 6], P('pipe', None, 'expert'), may hold values from 0 to 31, all different within a row; in each aligned block of 64 rows (0 to 63, 64 to 127, ..., all dimensions but the last counted through in order) at most 32 rows name the same one
- gate_values: float32 [1, 2, 2048, 6], P('pipe', None, 'expert'), may hold values from 0.1 to 0.5
- w_gate: bfloat16 [1, 32, 2048, 768], P('pipe', 'expert'), may hold values from -0.125 to 0.125
- w_up: bfloat16 [1, 32, 2048, 768], P('pipe', 'expert'), may hold values from -0.125 to 0.125
- w_down: bfloat16 [1, 32, 768, 2048], P('pipe', 'expert'), may hold values from -0.21875 to 0.21875
Outputs:
- received: bfloat16 [1, 2, 2048, 2048], P('pipe', None, 'expert')
- gate_grad: float32 [1, 2, 2048, 6], P('pipe', None, 'expert')
The draws below stay inside these ranges and needn't reach their ends.
Inputs may be any that keep to these rules, and one draw needn't show every extreme that they name: `expert_ids`: each row names 6 different experts. Within the 64 rows of one device for one section and micro-batch, no expert is named by more than 32 rows, a bound that some expert reaches in some of these blocks.
All inputs are finite; a program needn't handle non-finite values.
Results may differ from the reference program's by a relative error of at most 0.0041.
Values may be sent and summed in bfloat16 or wider, within the bound.
A program may use at most 128 MiB of HBM per device.

```python
import math
import jax
import jax.numpy as jnp
import numpy as np
from jax import lax

D = 2048
H = 768
TOP = 6
MB = 2
TOK_DEV = 64
SECTIONS = 1
EXPERTS = 32
TOKENS = 2048
CAP = 32


def block_levels(stream_key, dims, shards, least, high):
    def one(axis_at, shards_of):
        steps = jax.random.uniform(jax.random.fold_in(jax.random.fold_in(stream_key, 6), axis_at), (shards_of,), jnp.float32, least / len(shards), high / len(shards))
        return jnp.repeat(jnp.exp(steps), dims[axis_at] // shards_of).reshape((-1,) + (1,) * (len(dims) - axis_at - 1))

    gain = one(*shards[0])
    for cut in shards[1:]:
        gain = gain * one(*cut)
    return gain


def deal_out(stream_key, own, number, rows, amount, top, bound, lean):
    ranking = jax.random.permutation(stream_key, amount)
    packed, usual = shares(amount, rows * top, bound, lean, True), shares(amount, rows * top, bound, lean, False)
    places = jnp.arange(amount)

    def named(lengths, offset_by):
        used = int((lengths > 0).sum())
        fixed = max(1, used // 4)
        passed = fixed + (places - fixed + offset_by * (used - fixed)) % max(1, amount - fixed)
        return jnp.zeros((amount,), jnp.int32).at[ranking[jnp.where(places < fixed, places, passed)]].set(jnp.asarray(lengths, jnp.int32))

    lengths = jnp.where(number % 4 == 0, named(packed, number // 4), named(usual, number - number // 4 - 1))
    mixed = jax.random.permutation(jax.random.fold_in(own, 3), amount)
    source_of, taker = mixed[0:amount // 2 * 2:2], mixed[1:amount // 2 * 2:2]
    room = jnp.minimum(lengths[source_of] - 1, bound - lengths[taker]) // 2
    room = jnp.where((source_of == ranking[0]) | (taker == ranking[0]) | (lengths[taker] == 0), 0, jnp.maximum(room, 0))
    passed = jax.random.randint(jax.random.fold_in(own, 4), (amount // 2,), 0, 1 << 20) % (room + 1)
    lengths = lengths.at[source_of].add(-passed).at[taker].add(passed)
    members = jnp.searchsorted(jnp.cumsum(lengths), jnp.arange(rows * top), side="right").astype(jnp.int32)
    listing = members.reshape(top, rows).T
    listing = listing[jax.random.permutation(jax.random.fold_in(own, 1), rows)]
    offset_by = jax.random.randint(jax.random.fold_in(own, 2), (rows, 1), 0, top)
    return jnp.take_along_axis(listing, (jnp.arange(top)[None, :] + offset_by) % top, axis=1)


def shares(number_of, total, reach, slope, full):
    loads = [(1 << 20) // math.isqrt(standing ** slope) + 1 for standing in range(1, number_of + 1)]
    largest = reach if full else min(reach, max(-(-total // number_of), total * loads[0] // sum(loads)))
    least = 1 if total - largest >= number_of - 1 else 0
    holding, spare = [largest] + [least] * (number_of - 1), total - largest - least * (number_of - 1)
    while spare > 0:
        candidates = [i for i in range(1, number_of) if holding[i] < largest] or [i for i in range(1, number_of) if holding[i] < reach]
        mass, budget = sum([loads[i] for i in candidates]), spare
        for i in candidates:
            more = min(reach - holding[i], max(1, budget * loads[i] // mass), spare)
            holding[i] = holding[i] + more
            spare = spare - more
    return np.array(holding)


def centred(stream_key, shape, deviation, bound, split=(), kind=jnp.bfloat16):
    level = block_levels(stream_key, shape, split, -0.22, 0.18) if split else 1.0
    result = jax.random.normal(stream_key, shape, jnp.float32) * deviation * level
    return jnp.minimum(jnp.maximum(result, -bound), bound).astype(kind)


def setup_inputs(seed: int = 0) -> dict:
    seeds = jax.random.split(jax.random.key(seed), 8)
    inputs = centred(seeds[0], (SECTIONS, MB, TOKENS, D), 1.0, 6.0, ((2, 32),))
    grads_out = centred(seeds[1], (SECTIONS, MB, TOKENS, D), 1.0, 6.0, ((2, 32),))
    expert_ids_keys = jax.random.split(jax.random.fold_in(seeds[2], 1), SECTIONS * MB * TOKENS // TOK_DEV)
    expert_ids_turns = jax.random.permutation(jax.random.fold_in(seeds[2], 3), SECTIONS * MB * TOKENS // TOK_DEV)
    expert_ids = jax.vmap(lambda own, number: deal_out(jax.random.fold_in(seeds[2], 2), own, number, TOK_DEV, EXPERTS, TOP, CAP, 2))(expert_ids_keys, expert_ids_turns).reshape((SECTIONS, MB, TOKENS, TOP))
    gate_values = jnp.clip(0.1 + 0.4 * jax.random.uniform(seeds[3], (SECTIONS, MB, TOKENS, TOP), jnp.float32) ** block_levels(seeds[3], (SECTIONS, MB, TOKENS, TOP), ((2, 32),), -0.2, 0.2), 0.1, 0.5)
    w_gate = centred(seeds[4], (SECTIONS, EXPERTS, D, H), D ** -0.5, 0.125, ((1, 32),))
    w_up = centred(seeds[5], (SECTIONS, EXPERTS, D, H), D ** -0.5, 0.125, ((1, 32),))
    w_down = centred(seeds[6], (SECTIONS, EXPERTS, H, D), H ** -0.5, 0.21875, ((1, 32),))
    return {"inputs": inputs, "grads_out": grads_out, "expert_ids": expert_ids, "gate_values": gate_values, "w_gate": w_gate, "w_up": w_up, "w_down": w_down}


def expert_rows(x_rows, grad_rows, gate_weight, up_weight, down_weight):
    gate_pre = jnp.dot(x_rows, gate_weight, preferred_element_type=jnp.float32)
    up_pre = jnp.dot(x_rows, up_weight, preferred_element_type=jnp.float32)
    back_grad = lax.dot_general(grad_rows, down_weight, (((1,), (1,)), ((), ())), preferred_element_type=jnp.float32)
    logistic = jax.nn.sigmoid(gate_pre)
    swish = gate_pre * logistic
    score = jnp.sum(back_grad * swish * up_pre, axis=1).astype(jnp.bfloat16)
    d_gate = (back_grad * up_pre * logistic * (1.0 + gate_pre * (1.0 - logistic))).astype(jnp.bfloat16)
    d_up = (back_grad * swish).astype(jnp.bfloat16)
    pair_grad = lax.dot_general(d_gate, gate_weight, (((1,), (1,)), ((), ())), preferred_element_type=jnp.float32)
    pair_grad = pair_grad + lax.dot_general(d_up, up_weight, (((1,), (1,)), ((), ())), preferred_element_type=jnp.float32)
    return pair_grad.astype(jnp.bfloat16), score


def section_pass(x_rows, grad_rows, ids, gates, gate_all, up_all, down_all):
    pair_count = TOKENS * TOP
    block_rows = 128
    flat_ids = ids.reshape(pair_count).astype(jnp.int32)
    onehot = (flat_ids[:, None] == jnp.arange(EXPERTS, dtype=jnp.int32)[None, :]).astype(jnp.int32)
    counts = jnp.sum(onehot, axis=0).astype(jnp.int32)
    group_span = ((counts + block_rows - 1) // block_rows * block_rows).astype(jnp.int32)
    starts = (jnp.cumsum(group_span) - group_span).astype(jnp.int32)
    group_end = (starts + group_span).astype(jnp.int32)
    position = jnp.sum((jnp.cumsum(onehot, axis=0) - onehot) * onehot, axis=1).astype(jnp.int32)
    target = (starts[flat_ids] + position).astype(jnp.int32)
    buffer_rows = (pair_count // block_rows + EXPERTS + 1) * block_rows
    token_of = jnp.arange(pair_count, dtype=jnp.int32) // TOP
    buffer_x = jnp.zeros((buffer_rows, D), jnp.bfloat16).at[target].set(x_rows[token_of])
    buffer_grad = jnp.zeros((buffer_rows, D), jnp.bfloat16).at[target].set(grad_rows[token_of])
    block_count = buffer_rows // block_rows
    block_start = jnp.arange(block_count, dtype=jnp.int32) * block_rows
    owner_expert = jnp.sum((group_end[None, :] <= block_start[:, None]).astype(jnp.int32), axis=1).astype(jnp.int32)
    owner_expert = jnp.minimum(owner_expert, EXPERTS - 1).astype(jnp.int32)

    def one_block(index):
        first_row = (index * block_rows).astype(jnp.int32)
        chosen = owner_expert[index]
        return expert_rows(lax.dynamic_slice_in_dim(buffer_x, first_row, block_rows, 0),
                           lax.dynamic_slice_in_dim(buffer_grad, first_row, block_rows, 0),
                           gate_all[chosen], up_all[chosen], down_all[chosen])

    block_grads, block_scores = lax.map(one_block, jnp.arange(block_count, dtype=jnp.int32))
    block_grads = block_grads.reshape(buffer_rows, D)
    block_scores = block_scores.reshape(buffer_rows)
    pair_grad = block_grads[target].reshape(TOKENS, TOP, D).astype(jnp.float32)
    pair_score = block_scores[target].reshape(TOKENS, TOP).astype(jnp.float32)
    input_grad = grad_rows.astype(jnp.float32) + jnp.sum(gates[:, :, None].astype(jnp.float32) * pair_grad, axis=1)
    return input_grad.astype(jnp.bfloat16), pair_score


def reference(inputs, grads_out, expert_ids, gate_values, w_gate, w_up, w_down):
    all_grads = []
    all_scores = []
    for section in range(SECTIONS):
        grad_list = []
        score_list = []
        for micro in range(MB):
            input_grad, pair_score = section_pass(inputs[section, micro], grads_out[section, micro],
                                                  expert_ids[section, micro], gate_values[section, micro],
                                                  w_gate[section], w_up[section], w_down[section])
            grad_list.append(input_grad)
            score_list.append(pair_score)
        all_grads.append(jnp.stack(grad_list))
        all_scores.append(jnp.stack(score_list))
    stacked = jnp.stack(all_grads)
    received = jnp.roll(stacked, -1, axis=0)
    return received, jnp.stack(all_scores)
```

```python
import functools

import jax
import jax.numpy as jnp
from jax import lax
from jax.experimental import pallas as pl
from jax.experimental.pallas import tpu as pltpu
from jax.sharding import PartitionSpec as P

LANES = 128
NT = (((1,), (1,)), ((), ()))


def section_kernel(
    layers, x_hbm, g_hbm, ids_hbm, gates_hbm, wg_hbm, wu_hbm, wd_hbm,
    out_ref, score_ref, gathered,
    wg, wu, wd, xv, acc, staged, plane_in, diag_in, layer_out, layer_in, ids, gates, gate_block,
    w_loc, w_send, w_recv, loc,
    z_send, z_recv, zb_send, zb_recv, a_send, a_recv, b_send, b_recv,
    f_send, f_recv, fb_send, fb_recv, r_send, r_recv, l_send, l_recv,
):
    me = lax.axis_index("expert")
    experts = layers * 8
    z, place = me // 8, me % 8
    y, x, core = place // 4, (place // 2) % 2, place % 2
    micro, part, width = x_hbm.shape
    picks = ids.shape[2]
    rows = micro * part
    many = 4 * rows
    half = rows // 2
    late = rows // 4
    early = rows - late

    def at(layer, row, column, side):
        return ((layer * 2 + row) * 2 + column) * 2 + side

    partner = at(z, y, x, 1 - core)
    peers = [at(z, y, 1 - x, core), at(z, 1 - y, x, core)]

    def in_column(layer):
        return at(layer, y, x, core)

    upper = z // (layers // 2)
    depth = z + upper * (layers - 1 - 2 * z)

    def layer_of(t):
        over = (t - 2 * depth - 1 + 4 * layers) // (4 * layers)
        odd = t % 2
        near = odd * (depth - (t + 1) // 2) + (1 - odd) * (depth + t // 2)
        found = over * t + (1 - over) * near
        return found + upper * (layers - 1 - 2 * found)

    def remote(src, dst, send, recv, device):
        return pltpu.make_async_remote_copy(
            src_ref=src, dst_ref=dst, send_sem=send, recv_sem=recv,
            device_id={"expert": device}, device_id_type=pl.DeviceIdType.MESH,
        )

    first_rows, last_rows = pl.ds(0, early), pl.ds(early, late)

    def weight_copy(i):
        return remote(
            (wg_hbm, wu_hbm, wd_hbm)[i], (wg, wu, wd)[i].at[1], w_send.at[i], w_recv.at[i], partner
        )

    def weight_local(i):
        return pltpu.make_async_copy(
            (wg_hbm, wu_hbm, wd_hbm)[i], (wg, wu, wd)[i].at[0], w_loc.at[i]
        )

    def column_gather(layer, way):
        to = in_column((z + 2 * way - 1 + layers) % layers)
        part_at = gathered.at[layer, 0, first_rows]
        return remote(part_at, part_at, z_send.at[layer, way], z_recv.at[layer], to)

    def group_gather(layer, way):
        to = in_column((z + 2 * way - 1 + layers) % layers)
        part_at = gathered.at[layer, :, last_rows]
        return remote(part_at, part_at, zb_send.at[layer, way], zb_recv.at[layer], to)

    def plane_gather(layer, side):
        return remote(
            gathered.at[layer, 0, first_rows], gathered.at[layer, 1 + side, first_rows],
            a_send.at[layer, side], a_recv.at[layer, side], peers[side],
        )

    def plane_group(side):
        return remote(
            gathered.at[z, 0, last_rows], gathered.at[z, 1 + side, last_rows],
            b_send.at[side], b_recv.at[side], peers[side],
        )

    def forward(layer, side):
        mine = pl.ds(side * (early // 2), early // 2)
        return remote(
            gathered.at[layer, 1 + side, mine], gathered.at[layer, 3, mine],
            f_send.at[layer, side], f_recv.at[layer, side], peers[1 - side],
        )

    def forward_group(side):
        mine = pl.ds(early + side * (late // 2), late // 2)
        return remote(
            gathered.at[z, 1 + side, mine], gathered.at[z, 3, mine],
            fb_send.at[side], fb_recv.at[side], peers[1 - side],
        )

    def slot_of(t):
        if isinstance(t, int):
            return 0 if t == 0 else 1 + t % 2
        return 1 + t % 2

    def plane_reduce(t, k):
        return remote(
            staged.at[slot_of(t), 1 + k], plane_in.at[t, k],
            r_send.at[t, k], r_recv.at[t, k], peers[k],
        )

    def diag_reduce(t, side):
        return remote(
            staged.at[slot_of(t), 3, pl.ds(side * half, half)], diag_in.at[t, side],
            r_send.at[t, 2 + side], r_recv.at[t, 2 + side], peers[side],
        )

    def layer_reduce(t):
        return remote(
            layer_out.at[t], layer_in.at[z], l_send.at[t], l_recv.at[z], in_column(layer_of(t))
        )

    def layer_arrival(layer):
        return remote(
            layer_out.at[1], layer_in.at[layer], l_send.at[1], l_recv.at[layer], in_column(layer)
        )

    def passes(layer, way):
        if way == 1:
            return jnp.logical_and(layer < z, z < layers - 1)
        return jnp.logical_and(layer > z, z > 0)

    def relayed(layer):
        return jnp.logical_or(passes(layer, 0), passes(layer, 1))

    def relay(copy, layer):
        @pl.when(relayed(layer))
        def _():
            copy(layer, 0).wait_recv()
            for way in range(2):
                @pl.when(passes(layer, way))
                def _():
                    copy(layer, way).start()

    def arrive(copy, layer):
        @pl.when(jnp.logical_not(relayed(layer)))
        def _():
            copy(layer, 0).wait_recv()

    def both_ways(copy):
        @pl.when(z < layers - 1)
        def _():
            copy(z, 1).start()

        @pl.when(z > 0)
        def _():
            copy(z, 0).start()

    barrier = pltpu.get_barrier_semaphore()
    greeted = [partner] + peers + [in_column((z + s) % layers) for s in range(1, layers)]
    for device in greeted:
        pl.semaphore_signal(
            barrier, inc=1, device_id={"expert": device}, device_id_type=pl.DeviceIdType.MESH
        )
    local = [
        pltpu.make_async_copy(ids_hbm, ids, loc.at[0]),
        pltpu.make_async_copy(gates_hbm, gates, loc.at[1]),
    ]
    for m in range(micro):
        for i, source in enumerate((x_hbm, g_hbm)):
            local.append(
                pltpu.make_async_copy(
                    source.at[m],
                    gathered.at[z, 0, pl.ds(m * part, part), pl.ds(i * width, width)],
                    loc.at[2 + 2 * m + i],
                )
            )
    for copy in local:
        copy.start()
    for i in range(3):
        weight_local(i).start()
    lane = lax.broadcasted_iota(jnp.int32, (part, LANES), 1)
    wrapped = jnp.where(lane >= experts, lane - experts, lane)
    for copy in local[:2]:
        copy.wait()
    for m in range(micro):
        dense = jnp.zeros((part, LANES), jnp.float32)
        for k in range(picks):
            dense = dense + jnp.where(
                wrapped == ids[m, :, k : k + 1], gates[m, :, k : k + 1], 0.0
            )
        high = dense.astype(jnp.bfloat16).astype(jnp.float32)
        both = jnp.where(lane < experts, high, dense - high)
        gate_block[pl.ds(m * part, part), :] = both.astype(jnp.bfloat16)
    last = pltpu.make_async_copy(
        gate_block, gathered.at[z, 0, :, pl.ds(2 * width, LANES)], loc.at[0]
    )
    last.start()
    for copy in local[2:]:
        copy.wait()
    last.wait()
    pl.semaphore_wait(barrier, len(greeted))

    both_ways(column_gather)
    for side in range(2):
        plane_gather(z, side).start()
    for side in range(2):
        plane_group(side).start()
    for i in range(3):
        weight_copy(i).start()

    relay(column_gather, layer_of(1))
    relay(column_gather, layer_of(2))
    arrive(column_gather, layer_of(1))
    for side in range(2):
        plane_gather(layer_of(1), side).start()
    for side in range(2):
        plane_gather(z, side).wait_recv()
        forward(z, side).start()
    for side in range(2):
        plane_group(side).wait_recv()
        forward_group(side).start()
    for side in range(2):
        forward_group(side).wait_recv()
    both_ways(group_gather)
    relay(column_gather, layer_of(3))
    arrive(column_gather, layer_of(2))
    for side in range(2):
        plane_gather(layer_of(2), side).start()
    for i in range(3):
        weight_local(i).wait()

    lanes = lax.broadcasted_iota(jnp.int32, (many, LANES), 1)

    def expert(j, expert_id, slot):
        xs = xv[:, :, :width].reshape(many, width)
        gs = xv[:, :, width : 2 * width].reshape(many, width)
        gate_pre = jnp.dot(xs, wg[j], preferred_element_type=jnp.float32)
        up_pre = jnp.dot(xs, wu[j], preferred_element_type=jnp.float32)
        back = lax.dot_general(gs, wd[j], NT, preferred_element_type=jnp.float32)
        logistic = 1.0 / (1.0 + jnp.exp(-gate_pre))
        swish = gate_pre * logistic
        d_up = back * swish
        score = jnp.sum(d_up * up_pre, axis=1, keepdims=True)
        d_gate = (back * up_pre * logistic * (1.0 + gate_pre * (1.0 - logistic)))
        d_gate, d_up = d_gate.astype(jnp.bfloat16), d_up.astype(jnp.bfloat16)
        values = xv[:, :, 2 * width :].astype(jnp.float32).reshape(many, LANES)
        named = jnp.logical_or(lanes == expert_id, lanes == expert_id + experts)
        gate = jnp.sum(jnp.where(named, values, 0.0), axis=1, keepdims=True)
        spread = jnp.where(lanes == expert_id, score, 0.0)
        tile = min(512, width)
        for col in range(0, width, tile):
            cols = pl.ds(col, tile)
            pair = lax.dot_general(d_gate, wg[j, cols, :], NT, preferred_element_type=jnp.float32)
            pair = pair + lax.dot_general(
                d_up, wu[j, cols, :], NT, preferred_element_type=jnp.float32
            )
            pair = gate * pair.astype(jnp.bfloat16).astype(jnp.float32)
            if j == 0:
                acc[:, cols] = pair
            else:
                staged[slot, :, :, cols] = (
                    (acc[:, cols] + pair).astype(jnp.bfloat16).reshape(4, rows, tile)
                )
        cols = pl.ds(width, LANES)
        if j == 0:
            acc[:, cols] = spread
        else:
            staged[slot, :, :, cols] = (
                (acc[:, cols] + spread).astype(jnp.bfloat16).reshape(4, rows, LANES)
            )

    def start_diag(t):
        for side in range(2):
            diag_reduce(t, side).start()

    def merge_plane(t):
        for side in range(2):
            diag_reduce(t, side).wait_send()
            diag_reduce(t, side).wait_recv()
            mine = pl.ds(side * half, half)
            merged = staged[slot_of(t), 2 - side, mine].astype(jnp.float32)
            merged = merged + diag_in[t, side].astype(jnp.float32)
            staged[slot_of(t), 2 - side, mine] = merged.astype(jnp.bfloat16)
            plane_reduce(t, 1 - side).start()

    def plane_total(t):
        for k in range(2):
            plane_reduce(t, k).wait_send()
            plane_reduce(t, k).wait_recv()
        total = staged[slot_of(t), 0].astype(jnp.float32)
        for k in range(2):
            total = total + plane_in[t, k].astype(jnp.float32)
        return total

    def finish_plane(t):
        layer_out[t] = plane_total(t).astype(jnp.bfloat16)
        layer_reduce(t).start()

    def one_step(t, carry):
        layer = layer_of(t)
        following = layer_of(t + 1)

        @pl.when(t > 0)
        def _():
            arrive(group_gather, layer)

        for side in range(2):
            forward(layer, side).wait_recv()
        load = pltpu.make_async_copy(gathered.at[layer], xv, loc.at[1])
        load.start()
        load.wait()
        expert(0, me, 0)

        @pl.when(t + 1 < layers)
        def _():
            for side in range(2):
                plane_gather(following, side).wait_recv()
                forward(following, side).start()
            relay(group_gather, following)

        @pl.when(t == 0)
        def _():
            for i in range(3):
                weight_copy(i).wait_recv()

        @pl.when(t > 2)
        def _():
            finish_plane(t - 2)

        @pl.when(t > 1)
        def _():
            merge_plane(t - 1)

        slot = (t + layers - 1) // layers * (1 + t % 2)
        expert(1, partner, slot)

        @pl.when(t > 0)
        def _():
            start_diag(t)

        @pl.when(t + 4 < layers)
        def _():
            relay(column_gather, layer_of(t + 4))

        @pl.when(t + 3 < layers)
        def _():
            arrive(column_gather, layer_of(t + 3))
            for side in range(2):
                plane_gather(layer_of(t + 3), side).start()

        return carry

    lax.fori_loop(0, layers, one_step, 0)
    start_diag(0)
    finish_plane(layers - 2)
    merge_plane(layers - 1)
    merge_plane(0)
    finish_plane(layers - 1)
    own = xv.at[0]
    grads = pltpu.make_async_copy(gathered.at[z, 0], own, loc.at[0])
    grads.start()
    total = plane_total(0)
    for s in range(1, layers):
        layer = layer_of(s)
        layer_arrival(layer).wait_recv()
        total = total + layer_in[layer].astype(jnp.float32)
    grads.wait()
    for m in range(micro):
        mine = pl.ds(m * part, part)
        own_grad = xv[0, mine, width : 2 * width].astype(jnp.float32)
        some = total[m * part : (m + 1) * part]
        out_ref[m] = (own_grad + some[:, :width]).astype(jnp.bfloat16)
        scores = some[:, width:].astype(jnp.bfloat16).astype(jnp.float32)
        for k in range(picks):
            chosen = jnp.where(lane == ids[m, :, k : k + 1], scores, 0.0)
            score_ref[m, :, k : k + 1] = jnp.sum(chosen, axis=1, keepdims=True)

    for i in range(3):
        weight_copy(i).wait_send()
    for side in range(2):
        plane_group(side).wait_send()
        forward_group(side).wait_send()
    for copy in (column_gather, group_gather):
        @pl.when(z < layers - 1)
        def _():
            copy(z, 1).wait_send()

        @pl.when(z > 0)
        def _():
            copy(z, 0).wait_send()

    def settle(s, carry):
        layer = layer_of(s)
        for side in range(2):
            plane_gather(layer, side).wait_send()
            forward(layer, side).wait_send()

        @pl.when(s > 0)
        def _():
            layer_reduce(s).wait_send()
            for copy in (column_gather, group_gather):
                for way in range(2):
                    @pl.when(passes(layer, way))
                    def _():
                        copy(layer, way).wait_send()

        return carry

    lax.fori_loop(0, layers, settle, 0)


def section(inputs, grads, ids, gates, w_gate, w_up, w_down, experts):
    layers = experts // 8
    micro, part, width = inputs.shape
    picks = ids.shape[2]
    rows = micro * part
    hidden = w_gate.shape[1]
    wide, back = 2 * width + LANES, width + LANES
    bf16 = jnp.bfloat16
    sem = pltpu.SemaphoreType.DMA
    anywhere = pl.BlockSpec(memory_space=pl.ANY)
    vmem = pl.BlockSpec(memory_space=pltpu.VMEM)
    out, score, _ = pl.pallas_call(
        functools.partial(section_kernel, layers),
        in_specs=[anywhere] * 7,
        out_specs=[vmem, vmem, anywhere],
        out_shape=[
            jax.ShapeDtypeStruct((micro, part, width), bf16),
            jax.ShapeDtypeStruct((micro, part, picks), jnp.float32),
            jax.ShapeDtypeStruct((layers, 4, rows, wide), bf16),
        ],
        scratch_shapes=[
            pltpu.VMEM((2, width, hidden), bf16),
            pltpu.VMEM((2, width, hidden), bf16),
            pltpu.VMEM((2, hidden, width), bf16),
            pltpu.VMEM((4, rows, wide), bf16),
            pltpu.VMEM((4 * rows, back), jnp.float32),
            pltpu.VMEM((3, 4, rows, back), bf16),
            pltpu.VMEM((layers, 2, rows, back), bf16),
            pltpu.VMEM((layers, 2, rows // 2, back), bf16),
            pltpu.VMEM((layers, rows, back), bf16),
            pltpu.VMEM((layers, rows, back), bf16),
            pltpu.VMEM((micro, part, picks), jnp.int32),
            pltpu.VMEM((micro, part, picks), jnp.float32),
            pltpu.VMEM((rows, LANES), bf16),
            sem((3,)), sem((3,)), sem((3,)), sem((2 + 2 * micro,)),
            sem((layers, 2)), sem((layers,)), sem((layers, 2)), sem((layers,)),
            sem((layers, 2)), sem((layers, 2)), sem((2,)), sem((2,)),
            sem((layers, 2)), sem((layers, 2)), sem((2,)), sem((2,)),
            sem((layers, 4)), sem((layers, 4)),
            sem((layers,)), sem((layers,)),
        ],
        compiler_params=pltpu.CompilerParams(
            collective_id=0, has_side_effects=True, vmem_limit_bytes=63 * 1024 * 1024
        ),
    )(inputs, grads, ids, gates, w_gate, w_up, w_down)
    return out, score


def on_device(inputs, grads_out, expert_ids, gate_values, w_gate, w_up, w_down):
    out, score = section(
        inputs[0], grads_out[0], expert_ids[0], gate_values[0],
        w_gate[0, 0], w_up[0, 0], w_down[0, 0], lax.axis_size("expert"),
    )
    received, gate_grad = out[None], score[None]
    sections = lax.axis_size("pipe")
    if sections > 1:
        received = lax.ppermute(
            received, "pipe", [(s, (s - 1) % sections) for s in range(sections)]
        )
    return (received, gate_grad)


def solution(mesh):
    tokens = P("pipe", None, "expert", None)
    weights = P("pipe", "expert", None, None)
    return jax.shard_map(
        on_device,
        mesh=mesh,
        in_specs=(tokens,) * 4 + (weights,) * 3,
        out_specs=(tokens, tokens),
        check_vma=False,
    )
```

```python
import functools

import jax
import jax.numpy as jnp
from jax import lax
from jax.experimental import pallas as pl
from jax.experimental.pallas import tpu as pltpu
from jax.sharding import PartitionSpec as P

LANES = 128
NT = (((1,), (1,)), ((), ()))


def section_kernel(
    layers, x_hbm, g_hbm, ids_hbm, gates_hbm, wg_hbm, wu_hbm, wd_hbm,
    out_ref, score_ref, gathered, layer_in, group_in,
    wg, wu, wd, xv, acc, staged, plane_in, diag_in, layer_out, ids, gates,
    w_loc, w_send, w_recv, loc,
    z_send, z_recv, zb_send, zb_recv, a_send, a_recv, b_send, b_recv,
    f_send, f_recv, fb_send, fb_recv, r_send, r_recv, l_send, l_recv,
    g_send, g_recv,
):
    me = lax.axis_index("expert")
    experts = layers * 8
    z, place = me // 8, me % 8
    y, x, core = place // 4, (place // 2) % 2, place % 2
    micro, part, width = x_hbm.shape
    picks = ids.shape[0]
    rows = micro * part
    many = 4 * rows
    half = rows // 2
    late = rows // 4
    early = rows - late

    def at(layer, row, column, side):
        return ((layer * 2 + row) * 2 + column) * 2 + side

    partner = at(z, y, x, 1 - core)
    peers = [at(z, y, 1 - x, core), at(z, 1 - y, x, core)]

    def in_column(layer):
        return at(layer, y, x, core)

    upper = z // (layers // 2)
    depth = z + upper * (layers - 1 - 2 * z)

    def layer_of(t):
        over = (t - 2 * depth - 1 + 4 * layers) // (4 * layers)
        odd = t % 2
        near = odd * (depth + (t + 1) // 2) + (1 - odd) * (depth - t // 2)
        found = over * t + (1 - over) * near
        return found + upper * (layers - 1 - 2 * found)

    def remote(src, dst, send, recv, device):
        return pltpu.make_async_remote_copy(
            src_ref=src, dst_ref=dst, send_sem=send, recv_sem=recv,
            device_id={"expert": device}, device_id_type=pl.DeviceIdType.MESH,
        )

    first_rows, last_rows = pl.ds(0, early), pl.ds(early, late)

    def weight_copy(i):
        return remote(
            (wg_hbm, wu_hbm, wd_hbm)[i], (wg, wu, wd)[i].at[1], w_send.at[i], w_recv.at[i], partner
        )

    def weight_local(i):
        return pltpu.make_async_copy(
            (wg_hbm, wu_hbm, wd_hbm)[i], (wg, wu, wd)[i].at[0], w_loc.at[i]
        )

    def column_gather(layer, way, source=None):
        to = in_column((z + 2 * way - 1 + layers) % layers)
        part_at = gathered.at[layer, 0, first_rows]
        return remote(
            part_at if source is None else source, part_at,
            z_send.at[layer, way], z_recv.at[layer], to,
        )

    def group_gather(layer, way):
        to = in_column((z + 2 * way - 1 + layers) % layers)
        part_at = gathered.at[layer, :, last_rows]
        return remote(part_at, part_at, zb_send.at[layer, way], zb_recv.at[layer], to)

    def plane_gather(layer, side, source=None):
        return remote(
            gathered.at[layer, 0, first_rows] if source is None else source, gathered.at[layer, 1 + side, first_rows],
            a_send.at[layer, side], a_recv.at[layer, side], peers[side],
        )

    def plane_group(side):
        return remote(
            xv.at[0, last_rows], gathered.at[z, 1 + side, last_rows],
            b_send.at[side], b_recv.at[side], peers[side],
        )

    def forward(layer, side):
        mine = pl.ds(side * (early // 2), early // 2)
        return remote(
            gathered.at[layer, 1 + side, mine], gathered.at[layer, 3, mine],
            f_send.at[layer, side], f_recv.at[layer, side], peers[1 - side],
        )

    def forward_group(side):
        mine = pl.ds(early + side * (late // 2), late // 2)
        return remote(
            gathered.at[z, 1 + side, mine], gathered.at[z, 3, mine],
            fb_send.at[side], fb_recv.at[side], peers[1 - side],
        )

    def slot_of(t):
        if isinstance(t, int):
            return t if t < 2 else 2 + t % 2
        return 2 + t % 2

    def plane_reduce(t, k):
        return remote(
            staged.at[slot_of(t), 1 + k], plane_in.at[t, k],
            r_send.at[t, k], r_recv.at[t, k], peers[k],
        )

    def diag_reduce(t, side):
        return remote(
            staged.at[slot_of(t), 3, pl.ds(side * half, half)], diag_in.at[t, side],
            r_send.at[t, 2 + side], r_recv.at[t, 2 + side], peers[side],
        )

    def layer_reduce(t):
        return remote(
            layer_out.at[t], layer_in.at[z], l_send.at[t], l_recv.at[z], in_column(layer_of(t))
        )

    def layer_arrival(layer):
        return remote(
            layer_out.at[2], layer_in.at[layer], l_send.at[2], l_recv.at[layer], in_column(layer)
        )

    central = depth // (layers // 2 - 1)

    def group_reduce(kind):
        return remote(
            staged.at[1], group_in.at[kind], g_send.at[0], g_recv.at[kind],
            in_column(layer_of(1)),
        )

    def passes(layer, way):
        if way == 1:
            return jnp.logical_and(layer < z, z < layers - 1)
        return jnp.logical_and(layer > z, z > 0)

    def relayed(layer):
        return jnp.logical_or(passes(layer, 0), passes(layer, 1))

    def relay(copy, layer):
        @pl.when(relayed(layer))
        def _():
            copy(layer, 0).wait_recv()
            for way in range(2):
                @pl.when(passes(layer, way))
                def _():
                    copy(layer, way).start()

    def arrive(copy, layer):
        @pl.when(jnp.logical_not(relayed(layer)))
        def _():
            copy(layer, 0).wait_recv()

    def both_ways(act):
        @pl.when(z < layers - 1)
        def _():
            act(1)

        @pl.when(z > 0)
        def _():
            act(0)

    barrier = pltpu.get_barrier_semaphore()
    greeted = [partner] + peers + [in_column((z + s) % layers) for s in range(1, layers)]
    for device in greeted:
        pl.semaphore_signal(
            barrier, inc=1, device_id={"expert": device}, device_id_type=pl.DeviceIdType.MESH
        )
    own = xv.at[0]
    local = [
        pltpu.make_async_copy(ids_hbm, ids, loc.at[0]),
        pltpu.make_async_copy(gates_hbm, gates, loc.at[1]),
    ]
    for m in range(micro):
        for i, source in enumerate((x_hbm, g_hbm)):
            local.append(
                pltpu.make_async_copy(
                    source.at[m], own.at[pl.ds(m * part, part), pl.ds(i * width, width)],
                    loc.at[2 + 2 * m + i],
                )
            )
    for copy in local:
        copy.start()
    for i in range(3):
        weight_local(i).start()
    for copy in local[:2]:
        copy.wait()

    def pick_row(k):
        return [
            jnp.concatenate([ref[k, m : m + 1, :] for m in range(micro)], axis=1)
            for ref in (ids, gates)
        ]

    entry = lax.broadcasted_iota(jnp.int32, (LANES, rows), 0)
    wrapped = jnp.where(entry >= experts, entry - experts, entry)
    dense = jnp.zeros((LANES, rows), jnp.float32)
    for k in range(picks):
        names, values = pick_row(k)
        dense = dense + jnp.where(wrapped == names, values, 0.0)
    high = dense.astype(jnp.bfloat16).astype(jnp.float32)
    both = jnp.where(entry < experts, high, dense - high)
    xv[0, :, pl.ds(2 * width, LANES)] = both.T.astype(jnp.bfloat16)
    for copy in local[2:]:
        copy.wait()
    keep = pltpu.make_async_copy(
        own.at[last_rows], gathered.at[z, 0, last_rows], loc.at[0]
    )
    keep.start()
    pl.semaphore_wait(barrier, len(greeted))

    mine = xv.at[0, first_rows]
    both_ways(lambda way: column_gather(z, way, mine).start())
    for side in range(2):
        plane_gather(z, side, mine).start()
    for side in range(2):
        plane_group(side).start()
    for i in range(3):
        weight_copy(i).start()

    relay(column_gather, layer_of(1))
    relay(column_gather, layer_of(2))
    arrive(column_gather, layer_of(1))
    for side in range(2):
        plane_gather(layer_of(1), side).start()
    for side in range(2):
        plane_gather(z, side).wait_recv()
        forward(z, side).start()
    for side in range(2):
        plane_group(side).wait_recv()
        forward_group(side).start()
    for side in range(2):
        forward_group(side).wait_recv()
    keep.wait()
    both_ways(lambda way: group_gather(z, way).start())
    relay(column_gather, layer_of(3))
    arrive(column_gather, layer_of(2))
    for side in range(2):
        plane_gather(layer_of(2), side).start()
    for i in range(3):
        weight_local(i).wait()

    lanes = lax.broadcasted_iota(jnp.int32, (many, LANES), 1)

    def expert(j, expert_id, slot):
        xs = xv[:, :, :width].reshape(many, width)
        gs = xv[:, :, width : 2 * width].reshape(many, width)
        gate_pre = jnp.dot(xs, wg[j], preferred_element_type=jnp.float32)
        up_pre = jnp.dot(xs, wu[j], preferred_element_type=jnp.float32)
        back = lax.dot_general(gs, wd[j], NT, preferred_element_type=jnp.float32)
        logistic = 1.0 / (1.0 + jnp.exp(-gate_pre))
        swish = gate_pre * logistic
        d_up = back * swish
        score = jnp.sum(d_up * up_pre, axis=1, keepdims=True)
        d_gate = (back * up_pre * logistic * (1.0 + gate_pre * (1.0 - logistic)))
        d_gate, d_up = d_gate.astype(jnp.bfloat16), d_up.astype(jnp.bfloat16)
        values = xv[:, :, 2 * width :].astype(jnp.float32).reshape(many, LANES)
        named = jnp.logical_or(lanes == expert_id, lanes == expert_id + experts)
        gate = jnp.sum(jnp.where(named, values, 0.0), axis=1, keepdims=True)
        spread = jnp.where(lanes == expert_id, score, 0.0)
        tile = min(512, width)
        for col in range(0, width, tile):
            cols = pl.ds(col, tile)
            pair = lax.dot_general(d_gate, wg[j, cols, :], NT, preferred_element_type=jnp.float32)
            pair = pair + lax.dot_general(
                d_up, wu[j, cols, :], NT, preferred_element_type=jnp.float32
            )
            pair = gate * pair.astype(jnp.bfloat16).astype(jnp.float32)
            if j == 0:
                acc[:, cols] = pair
            else:
                staged[slot, :, :, cols] = (
                    (acc[:, cols] + pair).astype(jnp.bfloat16).reshape(4, rows, tile)
                )
        cols = pl.ds(width, LANES)
        if j == 0:
            acc[:, cols] = spread
        else:
            staged[slot, :, :, cols] = (
                (acc[:, cols] + spread).astype(jnp.bfloat16).reshape(4, rows, LANES)
            )

    def start_diag(t):
        for side in range(2):
            diag_reduce(t, side).start()

    def merge_plane(t):
        for side in range(2):
            diag_reduce(t, side).wait_send()
            diag_reduce(t, side).wait_recv()
            mine = pl.ds(side * half, half)
            merged = staged[slot_of(t), 2 - side, mine].astype(jnp.float32)
            merged = merged + diag_in[t, side].astype(jnp.float32)
            staged[slot_of(t), 2 - side, mine] = merged.astype(jnp.bfloat16)
            plane_reduce(t, 1 - side).start()

    def plane_total(t):
        for k in range(2):
            plane_reduce(t, k).wait_send()
            plane_reduce(t, k).wait_recv()
        total = staged[slot_of(t), 0].astype(jnp.float32)
        for k in range(2):
            total = total + plane_in[t, k].astype(jnp.float32)
        return total

    def finish_plane(t):
        layer_out[t] = plane_total(t).astype(jnp.bfloat16)
        layer_reduce(t).start()

    def one_step(t, carry):
        layer = layer_of(t)
        following = layer_of(t + 1)

        @pl.when(t > 0)
        def _():
            arrive(group_gather, layer)

        for side in range(2):
            forward(layer, side).wait_recv()
        others = pltpu.make_async_copy(
            gathered.at[layer, pl.ds(1, 3)], xv.at[pl.ds(1, 3)], loc.at[1]
        )
        others.start()

        @pl.when(t > 0)
        def _():
            first = pltpu.make_async_copy(gathered.at[layer, 0], own, loc.at[2])
            first.start()
            first.wait()

        others.wait()
        expert(0, me, 0)

        @pl.when(t + 1 < layers)
        def _():
            for side in range(2):
                plane_gather(following, side).wait_recv()
                forward(following, side).start()
            relay(group_gather, following)

        @pl.when(t == 0)
        def _():
            for i in range(3):
                weight_copy(i).wait_recv()
            both_ways(lambda way: column_gather(z, way, mine).wait_send())
            for side in range(2):
                plane_gather(z, side, mine).wait_send()
                plane_group(side).wait_send()

        @pl.when(t > 3)
        def _():
            finish_plane(t - 2)

        @pl.when(t > 2)
        def _():
            merge_plane(t - 1)

        later = (t + layers - 2) // layers
        slot = later * (2 + t % 2) + (1 - later) * t
        expert(1, partner, slot)

        @pl.when(t == 1)
        def _():
            group_reduce(central).start()

        @pl.when(t > 1)
        def _():
            start_diag(t)

        @pl.when(t + 4 < layers)
        def _():
            relay(column_gather, layer_of(t + 4))

        @pl.when(t + 3 < layers)
        def _():
            arrive(column_gather, layer_of(t + 3))
            for side in range(2):
                plane_gather(layer_of(t + 3), side).start()

        return carry

    lax.fori_loop(0, layers, one_step, 0)
    finish_plane(layers - 2)
    merge_plane(layers - 1)
    for kind, there in enumerate((depth > 0, central > 0)):
        @pl.when(there)
        def _():
            group_reduce(kind).wait_recv()
            load = pltpu.make_async_copy(
                group_in.at[kind], xv.at[:, :, pl.ds(0, width + LANES)], loc.at[0]
            )
            load.start()
            load.wait()
            for i in range(4):
                merged = staged[0, i].astype(jnp.float32)
                merged = merged + xv[i, :, : width + LANES].astype(jnp.float32)
                staged[0, i] = merged.astype(jnp.bfloat16)

    start_diag(0)
    finish_plane(layers - 1)
    merge_plane(0)
    grads = [
        pltpu.make_async_copy(g_hbm.at[m], out_ref.at[m], loc.at[m]) for m in range(micro)
    ]
    for copy in grads:
        copy.start()
    acc[pl.ds(0, rows), :] = jnp.zeros((rows, width + LANES), jnp.float32)

    def add_layer(s, carry):
        layer = layer_of(s)

        @pl.when(jnp.logical_or(s > 2, jnp.where(s == 1, central, depth) == 0))
        def _():
            layer_arrival(layer).wait_recv()
            landed = xv.at[0, :, pl.ds(0, width + LANES)]
            load = pltpu.make_async_copy(layer_in.at[layer], landed, loc.at[micro])
            load.start()
            load.wait()
            acc[pl.ds(0, rows), :] += landed[...].astype(jnp.float32)

        return carry

    lax.fori_loop(1, layers, add_layer, 0)
    total = acc[pl.ds(0, rows), :] + plane_total(0)
    for m in range(micro):
        grads[m].wait()
        some = total[m * part : (m + 1) * part, :width]
        out_ref[m] = (out_ref[m].astype(jnp.float32) + some).astype(jnp.bfloat16)
    scores = total[:, width:].astype(jnp.bfloat16).astype(jnp.float32).T
    for k in range(picks):
        names, _ = pick_row(k)
        chosen = jnp.sum(jnp.where(entry == names, scores, 0.0), axis=0, keepdims=True)
        for m in range(micro):
            score_ref[k, m : m + 1, :] = chosen[:, m * part : (m + 1) * part]

    for i in range(3):
        weight_copy(i).wait_send()
    for side in range(2):
        forward_group(side).wait_send()
        forward(z, side).wait_send()
    both_ways(lambda way: group_gather(z, way).wait_send())
    group_reduce(central).wait_send()

    def settle(s, carry):
        layer = layer_of(s)
        for side in range(2):
            plane_gather(layer, side).wait_send()
            forward(layer, side).wait_send()

        @pl.when(s > 1)
        def _():
            layer_reduce(s).wait_send()

        for copy in (column_gather, group_gather):
            for way in range(2):
                @pl.when(passes(layer, way))
                def _():
                    copy(layer, way).wait_send()

        return carry

    lax.fori_loop(1, layers, settle, 0)


def section(inputs, grads, ids, gates, w_gate, w_up, w_down, experts):
    layers = experts // 8
    micro, part, width = inputs.shape
    picks = ids.shape[0]
    rows = micro * part
    hidden = w_gate.shape[1]
    wide, back = 2 * width + LANES, width + LANES
    bf16 = jnp.bfloat16
    sem = pltpu.SemaphoreType.DMA
    anywhere = pl.BlockSpec(memory_space=pl.ANY)
    vmem = pl.BlockSpec(memory_space=pltpu.VMEM)
    out, score, *_ = pl.pallas_call(
        functools.partial(section_kernel, layers),
        in_specs=[anywhere] * 7,
        out_specs=[vmem, vmem] + [anywhere] * 3,
        out_shape=[
            jax.ShapeDtypeStruct((micro, part, width), bf16),
            jax.ShapeDtypeStruct((picks, micro, part), jnp.float32),
            jax.ShapeDtypeStruct((layers, 4, rows, wide), bf16),
            jax.ShapeDtypeStruct((layers, rows, back), bf16),
            jax.ShapeDtypeStruct((2, 4, rows, back), bf16),
        ],
        scratch_shapes=[
            pltpu.VMEM((2, width, hidden), bf16),
            pltpu.VMEM((2, width, hidden), bf16),
            pltpu.VMEM((2, hidden, width), bf16),
            pltpu.VMEM((4, rows, wide), bf16),
            pltpu.VMEM((4 * rows, back), jnp.float32),
            pltpu.VMEM((4, 4, rows, back), bf16),
            pltpu.VMEM((layers, 2, rows, back), bf16),
            pltpu.VMEM((layers, 2, rows // 2, back), bf16),
            pltpu.VMEM((layers, rows, back), bf16),
            pltpu.VMEM((picks, micro, part), jnp.int32),
            pltpu.VMEM((picks, micro, part), jnp.float32),
            sem((3,)), sem((3,)), sem((3,)), sem((2 + 2 * micro,)),
            sem((layers, 2)), sem((layers,)), sem((layers, 2)), sem((layers,)),
            sem((layers, 2)), sem((layers, 2)), sem((2,)), sem((2,)),
            sem((layers, 2)), sem((layers, 2)), sem((2,)), sem((2,)),
            sem((layers, 4)), sem((layers, 4)),
            sem((layers,)), sem((layers,)), sem((1,)), sem((2,)),
        ],
        compiler_params=pltpu.CompilerParams(
            collective_id=0, has_side_effects=True, vmem_limit_bytes=63 * 1024 * 1024
        ),
    )(inputs, grads, ids, gates, w_gate, w_up, w_down)
    return out, score


def on_device(inputs, grads_out, expert_ids, gate_values, w_gate, w_up, w_down):
    out, score = section(
        inputs[0], grads_out[0],
        jnp.transpose(expert_ids[0], (2, 0, 1)), jnp.transpose(gate_values[0], (2, 0, 1)),
        w_gate[0, 0], w_up[0, 0], w_down[0, 0], lax.axis_size("expert"),
    )
    received, gate_grad = out[None], jnp.transpose(score, (1, 2, 0))[None]
    sections = lax.axis_size("pipe")
    if sections > 1:
        received = lax.ppermute(
            received, "pipe", [(s, (s - 1) % sections) for s in range(sections)]
        )
    return (received, gate_grad)


def solution(mesh):
    tokens = P("pipe", None, "expert", None)
    weights = P("pipe", "expert", None, None)
    return jax.shard_map(
        on_device,
        mesh=mesh,
        in_specs=(tokens,) * 4 + (weights,) * 3,
        out_specs=(tokens, tokens),
        check_vma=False,
    )
```

```python
import functools

import jax
import jax.numpy as jnp
from jax import lax
from jax.experimental import pallas as pl
from jax.experimental.pallas import tpu as pltpu
from jax.sharding import PartitionSpec as P

LANES = 128
NT = (((1,), (1,)), ((), ()))


def section_kernel(
    layers, x_hbm, g_hbm, ids_hbm, gates_hbm, wg_hbm, wu_hbm, wd_hbm,
    out_ref, score_ref, gathered, layer_in, group_in,
    wg, wu, wd, xv, acc, staged, plane_in, diag_in, layer_out, ids, gates,
    w_loc, w_send, w_recv, loc,
    z_send, z_recv, zb_send, zb_recv, a_send, a_recv, b_send, b_recv,
    f_send, f_recv, fb_send, fb_recv, r_send, r_recv, l_send, l_recv,
    g_send, g_recv,
):
    me = lax.axis_index("expert")
    experts = layers * 8
    z, place = me // 8, me % 8
    y, x, core = place // 4, (place // 2) % 2, place % 2
    micro, part, width = x_hbm.shape
    picks = ids.shape[0]
    rows = micro * part
    many = 4 * rows
    half = rows // 2
    late = rows // 4
    early = rows - late

    def at(layer, row, column, side):
        return ((layer * 2 + row) * 2 + column) * 2 + side

    partner = at(z, y, x, 1 - core)
    peers = [at(z, y, 1 - x, core), at(z, 1 - y, x, core)]

    def in_column(layer):
        return at(layer, y, x, core)

    upper = z // (layers // 2)
    depth = z + upper * (layers - 1 - 2 * z)

    def layer_of(t):
        over = (t - 2 * depth - 1 + 4 * layers) // (4 * layers)
        odd = t % 2
        near = odd * (depth + (t + 1) // 2) + (1 - odd) * (depth - t // 2)
        found = over * t + (1 - over) * near
        return found + upper * (layers - 1 - 2 * found)

    def remote(src, dst, send, recv, device):
        return pltpu.make_async_remote_copy(
            src_ref=src, dst_ref=dst, send_sem=send, recv_sem=recv,
            device_id={"expert": device}, device_id_type=pl.DeviceIdType.MESH,
        )

    first_rows, last_rows = pl.ds(0, early), pl.ds(early, late)

    def weight_copy(i):
        return remote(
            (wg_hbm, wu_hbm, wd_hbm)[i], (wg, wu, wd)[i].at[1], w_send.at[i], w_recv.at[i], partner
        )

    def weight_local(i):
        return pltpu.make_async_copy(
            (wg_hbm, wu_hbm, wd_hbm)[i], (wg, wu, wd)[i].at[0], w_loc.at[i]
        )

    def column_gather(layer, way, source=None):
        to = in_column((z + 2 * way - 1 + layers) % layers)
        part_at = gathered.at[layer, 0, first_rows]
        return remote(
            part_at if source is None else source, part_at,
            z_send.at[layer, way], z_recv.at[layer], to,
        )

    def group_gather(layer, way):
        to = in_column((z + 2 * way - 1 + layers) % layers)
        part_at = gathered.at[layer, :, last_rows]
        return remote(part_at, part_at, zb_send.at[layer, way], zb_recv.at[layer], to)

    def plane_gather(layer, side, piece, own=False):
        mine = pl.ds((side + piece) % 2 * (early // 2), early // 2)
        return remote(
            xv.at[0, mine] if own else gathered.at[layer, 0, mine],
            gathered.at[layer, 1 + side, mine],
            a_send.at[layer, side, piece], a_recv.at[layer, side, piece], peers[side],
        )

    def start_plane(layer, own=False):
        for piece in range(2):
            for side in range(2):
                plane_gather(layer, side, piece, own).start()

    def start_forward(layer):
        for side in range(2):
            plane_gather(layer, side, 0).wait_recv()
            forward(layer, side).start()

    def plane_group(side):
        return remote(
            xv.at[0, last_rows], gathered.at[z, 1 + side, last_rows],
            b_send.at[side], b_recv.at[side], peers[side],
        )

    def forward(layer, side):
        mine = pl.ds(side * (early // 2), early // 2)
        return remote(
            gathered.at[layer, 1 + side, mine], gathered.at[layer, 3, mine],
            f_send.at[layer, side], f_recv.at[layer, side], peers[1 - side],
        )

    def forward_group(side):
        mine = pl.ds(early + side * (late // 2), late // 2)
        return remote(
            gathered.at[z, 1 + side, mine], gathered.at[z, 3, mine],
            fb_send.at[side], fb_recv.at[side], peers[1 - side],
        )

    def slot_of(t):
        if isinstance(t, int):
            return t if t < 2 else 2 + t % 2
        return 2 + t % 2

    def plane_reduce(t, k):
        return remote(
            staged.at[slot_of(t), 1 + k], plane_in.at[t, k],
            r_send.at[t, k], r_recv.at[t, k], peers[k],
        )

    def diag_reduce(t, side):
        return remote(
            staged.at[slot_of(t), 3, pl.ds(side * half, half)], diag_in.at[t, side],
            r_send.at[t, 2 + side], r_recv.at[t, 2 + side], peers[side],
        )

    def layer_reduce(t):
        return remote(
            layer_out.at[t], layer_in.at[z], l_send.at[t], l_recv.at[z], in_column(layer_of(t))
        )

    def layer_arrival(layer):
        return remote(
            layer_out.at[2], layer_in.at[layer], l_send.at[2], l_recv.at[layer], in_column(layer)
        )

    central = depth // (layers // 2 - 1)

    def group_reduce(kind):
        return remote(
            staged.at[1], group_in.at[kind], g_send.at[0], g_recv.at[kind],
            in_column(layer_of(1)),
        )

    def passes(layer, way):
        if way == 1:
            return jnp.logical_and(layer < z, z < layers - 1)
        return jnp.logical_and(layer > z, z > 0)

    def relayed(layer):
        return jnp.logical_or(passes(layer, 0), passes(layer, 1))

    def relay(copy, layer):
        @pl.when(relayed(layer))
        def _():
            copy(layer, 0).wait_recv()
            for way in range(2):
                @pl.when(passes(layer, way))
                def _():
                    copy(layer, way).start()

    def arrive(copy, layer):
        @pl.when(jnp.logical_not(relayed(layer)))
        def _():
            copy(layer, 0).wait_recv()

    def both_ways(act):
        @pl.when(z < layers - 1)
        def _():
            act(1)

        @pl.when(z > 0)
        def _():
            act(0)

    barrier = pltpu.get_barrier_semaphore()
    greeted = [partner] + peers + [in_column((z + s) % layers) for s in range(1, layers)]
    for device in greeted:
        pl.semaphore_signal(
            barrier, inc=1, device_id={"expert": device}, device_id_type=pl.DeviceIdType.MESH
        )
    own = xv.at[0]
    local = [
        pltpu.make_async_copy(ids_hbm, ids, loc.at[0]),
        pltpu.make_async_copy(gates_hbm, gates, loc.at[1]),
    ]
    for m in range(micro):
        for i, source in enumerate((x_hbm, g_hbm)):
            local.append(
                pltpu.make_async_copy(
                    source.at[m], own.at[pl.ds(m * part, part), pl.ds(i * width, width)],
                    loc.at[2 + 2 * m + i],
                )
            )
    for copy in local:
        copy.start()
    for i in range(3):
        weight_local(i).start()
    for copy in local[:2]:
        copy.wait()

    def pick_row(k):
        return [
            jnp.concatenate([ref[k, m : m + 1, :] for m in range(micro)], axis=1)
            for ref in (ids, gates)
        ]

    entry = lax.broadcasted_iota(jnp.int32, (LANES, rows), 0)
    wrapped = jnp.where(entry >= experts, entry - experts, entry)
    dense = jnp.zeros((LANES, rows), jnp.float32)
    for k in range(picks):
        names, values = pick_row(k)
        dense = dense + jnp.where(wrapped == names, values, 0.0)
    high = dense.astype(jnp.bfloat16).astype(jnp.float32)
    both = jnp.where(entry < experts, high, dense - high)
    xv[0, :, pl.ds(2 * width, LANES)] = both.T.astype(jnp.bfloat16)
    for copy in local[2:]:
        copy.wait()
    keep = pltpu.make_async_copy(
        own.at[last_rows], gathered.at[z, 0, last_rows], loc.at[0]
    )
    keep.start()
    pl.semaphore_wait(barrier, len(greeted))

    mine = xv.at[0, first_rows]
    both_ways(lambda way: column_gather(z, way, mine).start())
    for side in range(2):
        plane_group(side).start()
    start_plane(z, True)
    for i in range(3):
        weight_copy(i).start()
    for side in range(2):
        plane_group(side).wait_recv()
        forward_group(side).start()
    start_forward(z)
    relay(column_gather, layer_of(1))
    relay(column_gather, layer_of(2))
    arrive(column_gather, layer_of(1))
    start_plane(layer_of(1))
    for side in range(2):
        forward_group(side).wait_recv()
    keep.wait()
    both_ways(lambda way: group_gather(z, way).start())
    relay(column_gather, layer_of(3))
    arrive(column_gather, layer_of(2))
    start_forward(layer_of(1))
    start_plane(layer_of(2))
    for i in range(3):
        weight_local(i).wait()

    lanes = lax.broadcasted_iota(jnp.int32, (many, LANES), 1)

    def expert(j, expert_id, slot, between=lambda: None):
        xs = xv[:, :, :width].reshape(many, width)
        gs = xv[:, :, width : 2 * width].reshape(many, width)
        gate_pre = jnp.dot(xs, wg[j], preferred_element_type=jnp.float32)
        up_pre = jnp.dot(xs, wu[j], preferred_element_type=jnp.float32)
        back = lax.dot_general(gs, wd[j], NT, preferred_element_type=jnp.float32)
        logistic = 1.0 / (1.0 + jnp.exp(-gate_pre))
        swish = gate_pre * logistic
        d_up = back * swish
        score = jnp.sum(d_up * up_pre, axis=1, keepdims=True)
        d_gate = (back * up_pre * logistic * (1.0 + gate_pre * (1.0 - logistic)))
        d_gate, d_up = d_gate.astype(jnp.bfloat16), d_up.astype(jnp.bfloat16)
        values = xv[:, :, 2 * width :].astype(jnp.float32).reshape(many, LANES)
        named = jnp.logical_or(lanes == expert_id, lanes == expert_id + experts)
        gate = jnp.sum(jnp.where(named, values, 0.0), axis=1, keepdims=True)
        spread = jnp.where(lanes == expert_id, score, 0.0)
        between()
        tile = min(512, width)
        for col in range(0, width, tile):
            cols = pl.ds(col, tile)
            pair = lax.dot_general(d_gate, wg[j, cols, :], NT, preferred_element_type=jnp.float32)
            pair = pair + lax.dot_general(
                d_up, wu[j, cols, :], NT, preferred_element_type=jnp.float32
            )
            pair = gate * pair.astype(jnp.bfloat16).astype(jnp.float32)
            if j == 0:
                acc[:, cols] = pair
            else:
                staged[slot, :, :, cols] = (
                    (acc[:, cols] + pair).astype(jnp.bfloat16).reshape(4, rows, tile)
                )
        cols = pl.ds(width, LANES)
        if j == 0:
            acc[:, cols] = spread
        else:
            staged[slot, :, :, cols] = (
                (acc[:, cols] + spread).astype(jnp.bfloat16).reshape(4, rows, LANES)
            )

    def start_diag(t):
        for side in range(2):
            diag_reduce(t, side).start()

    def merge_plane(t):
        for side in range(2):
            diag_reduce(t, side).wait_send()
            diag_reduce(t, side).wait_recv()
            mine = pl.ds(side * half, half)
            merged = staged[slot_of(t), 2 - side, mine].astype(jnp.float32)
            merged = merged + diag_in[t, side].astype(jnp.float32)
            staged[slot_of(t), 2 - side, mine] = merged.astype(jnp.bfloat16)
            plane_reduce(t, 1 - side).start()

    def plane_total(t):
        for k in range(2):
            plane_reduce(t, k).wait_send()
            plane_reduce(t, k).wait_recv()
        total = staged[slot_of(t), 0].astype(jnp.float32)
        for k in range(2):
            total = total + plane_in[t, k].astype(jnp.float32)
        return total

    def finish_plane(t):
        layer_out[t] = plane_total(t).astype(jnp.bfloat16)
        layer_reduce(t).start()

    def one_step(t, carry):
        layer = layer_of(t)
        following = layer_of(t + 1)

        @pl.when(t > 0)
        def _():
            arrive(group_gather, layer)

        for side in range(2):
            plane_gather(layer, side, 1).wait_recv()
            forward(layer, side).wait_recv()
        others = pltpu.make_async_copy(
            gathered.at[layer, pl.ds(1, 3)], xv.at[pl.ds(1, 3)], loc.at[1]
        )
        others.start()

        @pl.when(t > 0)
        def _():
            first = pltpu.make_async_copy(gathered.at[layer, 0], own, loc.at[2])
            first.start()
            first.wait()

        others.wait()
        def sums():
            @pl.when(t > 3)
            def _():
                finish_plane(t - 2)

            @pl.when(t > 2)
            def _():
                merge_plane(t - 1)

        expert(0, me, 0, sums)

        @pl.when(t == 0)
        def _():
            relay(group_gather, layer_of(1))

        @pl.when(t + 2 < layers)
        def _():
            relay(group_gather, layer_of(t + 2))

        @pl.when(t == 0)
        def _():
            for i in range(3):
                weight_copy(i).wait_recv()
            both_ways(lambda way: column_gather(z, way, mine).wait_send())
            for side in range(2):
                plane_group(side).wait_send()
                for piece in range(2):
                    plane_gather(z, side, piece, True).wait_send()

        later = (t + layers - 2) // layers
        slot = later * (2 + t % 2) + (1 - later) * t
        expert(1, partner, slot)

        @pl.when(t == 1)
        def _():
            group_reduce(central).start()

        @pl.when(t > 1)
        def _():
            start_diag(t)

        @pl.when(t + 2 < layers)
        def _():
            start_forward(layer_of(t + 2))

        @pl.when(t + 4 < layers)
        def _():
            relay(column_gather, layer_of(t + 4))

        @pl.when(t + 3 < layers)
        def _():
            arrive(column_gather, layer_of(t + 3))
            start_plane(layer_of(t + 3))

        return carry

    lax.fori_loop(0, layers, one_step, 0)
    finish_plane(layers - 2)
    merge_plane(layers - 1)
    for kind, there in enumerate((depth > 0, central > 0)):
        @pl.when(there)
        def _():
            group_reduce(kind).wait_recv()
            load = pltpu.make_async_copy(
                group_in.at[kind], xv.at[:, :, pl.ds(0, width + LANES)], loc.at[0]
            )
            load.start()
            load.wait()
            for i in range(4):
                merged = staged[0, i].astype(jnp.float32)
                merged = merged + xv[i, :, : width + LANES].astype(jnp.float32)
                staged[0, i] = merged.astype(jnp.bfloat16)

    start_diag(0)
    finish_plane(layers - 1)
    merge_plane(0)
    grads = [
        pltpu.make_async_copy(g_hbm.at[m], out_ref.at[m], loc.at[m]) for m in range(micro)
    ]
    for copy in grads:
        copy.start()
    acc[pl.ds(0, rows), :] = jnp.zeros((rows, width + LANES), jnp.float32)

    def add_layer(s, carry):
        layer = layer_of(s)

        @pl.when(jnp.logical_or(s > 2, jnp.where(s == 1, central, depth) == 0))
        def _():
            layer_arrival(layer).wait_recv()
            landed = xv.at[0, :, pl.ds(0, width + LANES)]
            load = pltpu.make_async_copy(layer_in.at[layer], landed, loc.at[micro])
            load.start()
            load.wait()
            acc[pl.ds(0, rows), :] += landed[...].astype(jnp.float32)

        return carry

    lax.fori_loop(1, layers, add_layer, 0)
    total = acc[pl.ds(0, rows), :] + plane_total(0)
    for m in range(micro):
        grads[m].wait()
        some = total[m * part : (m + 1) * part, :width]
        out_ref[m] = (out_ref[m].astype(jnp.float32) + some).astype(jnp.bfloat16)
    scores = total[:, width:].astype(jnp.bfloat16).astype(jnp.float32).T
    for k in range(picks):
        names, _ = pick_row(k)
        chosen = jnp.sum(jnp.where(entry == names, scores, 0.0), axis=0, keepdims=True)
        for m in range(micro):
            score_ref[k, m : m + 1, :] = chosen[:, m * part : (m + 1) * part]

    for i in range(3):
        weight_copy(i).wait_send()
    for side in range(2):
        forward_group(side).wait_send()
        forward(z, side).wait_send()
    both_ways(lambda way: group_gather(z, way).wait_send())
    group_reduce(central).wait_send()

    def settle(s, carry):
        layer = layer_of(s)
        for side in range(2):
            for piece in range(2):
                plane_gather(layer, side, piece).wait_send()
            forward(layer, side).wait_send()

        @pl.when(s > 1)
        def _():
            layer_reduce(s).wait_send()

        for copy in (column_gather, group_gather):
            for way in range(2):
                @pl.when(passes(layer, way))
                def _():
                    copy(layer, way).wait_send()

        return carry

    lax.fori_loop(1, layers, settle, 0)


def section(inputs, grads, ids, gates, w_gate, w_up, w_down, experts):
    layers = experts // 8
    micro, part, width = inputs.shape
    picks = ids.shape[0]
    rows = micro * part
    hidden = w_gate.shape[1]
    wide, back = 2 * width + LANES, width + LANES
    bf16 = jnp.bfloat16
    sem = pltpu.SemaphoreType.DMA
    anywhere = pl.BlockSpec(memory_space=pl.ANY)
    vmem = pl.BlockSpec(memory_space=pltpu.VMEM)
    out, score, *_ = pl.pallas_call(
        functools.partial(section_kernel, layers),
        in_specs=[anywhere] * 7,
        out_specs=[vmem, vmem] + [anywhere] * 3,
        out_shape=[
            jax.ShapeDtypeStruct((micro, part, width), bf16),
            jax.ShapeDtypeStruct((picks, micro, part), jnp.float32),
            jax.ShapeDtypeStruct((layers, 4, rows, wide), bf16),
            jax.ShapeDtypeStruct((layers, rows, back), bf16),
            jax.ShapeDtypeStruct((2, 4, rows, back), bf16),
        ],
        scratch_shapes=[
            pltpu.VMEM((2, width, hidden), bf16),
            pltpu.VMEM((2, width, hidden), bf16),
            pltpu.VMEM((2, hidden, width), bf16),
            pltpu.VMEM((4, rows, wide), bf16),
            pltpu.VMEM((4 * rows, back), jnp.float32),
            pltpu.VMEM((4, 4, rows, back), bf16),
            pltpu.VMEM((layers, 2, rows, back), bf16),
            pltpu.VMEM((layers, 2, rows // 2, back), bf16),
            pltpu.VMEM((layers, rows, back), bf16),
            pltpu.VMEM((picks, micro, part), jnp.int32),
            pltpu.VMEM((picks, micro, part), jnp.float32),
            sem((3,)), sem((3,)), sem((3,)), sem((2 + 2 * micro,)),
            sem((layers, 2)), sem((layers,)), sem((layers, 2)), sem((layers,)),
            sem((layers, 2, 2)), sem((layers, 2, 2)), sem((2,)), sem((2,)),
            sem((layers, 2)), sem((layers, 2)), sem((2,)), sem((2,)),
            sem((layers, 4)), sem((layers, 4)),
            sem((layers,)), sem((layers,)), sem((1,)), sem((2,)),
        ],
        compiler_params=pltpu.CompilerParams(
            collective_id=0, has_side_effects=True, vmem_limit_bytes=63 * 1024 * 1024
        ),
    )(inputs, grads, ids, gates, w_gate, w_up, w_down)
    return out, score


def on_device(inputs, grads_out, expert_ids, gate_values, w_gate, w_up, w_down):
    out, score = section(
        inputs[0], grads_out[0],
        jnp.transpose(expert_ids[0], (2, 0, 1)), jnp.transpose(gate_values[0], (2, 0, 1)),
        w_gate[0, 0], w_up[0, 0], w_down[0, 0], lax.axis_size("expert"),
    )
    received, gate_grad = out[None], jnp.transpose(score, (1, 2, 0))[None]
    sections = lax.axis_size("pipe")
    if sections > 1:
        received = lax.ppermute(
            received, "pipe", [(s, (s - 1) % sections) for s in range(sections)]
        )
    return (received, gate_grad)


def solution(mesh):
    tokens = P("pipe", None, "expert", None)
    weights = P("pipe", "expert", None, None)
    return jax.shard_map(
        on_device,
        mesh=mesh,
        in_specs=(tokens,) * 4 + (weights,) * 3,
        out_specs=(tokens, tokens),
        check_vma=False,
    )
```

```python
import functools

import jax
import jax.numpy as jnp
from jax import lax
from jax.experimental import pallas as pl
from jax.experimental.pallas import tpu as pltpu
from jax.sharding import PartitionSpec as P

LANES = 128
NT = (((1,), (1,)), ((), ()))


def section_kernel(
    layers, x_hbm, g_hbm, ids_hbm, gates_hbm, wg_hbm, wu_hbm, wd_hbm,
    out_ref, score_ref, gathered, layer_in, group_in,
    wg, wu, wd, xv, acc, staged, plane_in, diag_in, layer_out, ids, gates,
    facts, spread, score_out, score_in, score_all,
    w_loc, w_send, w_recv, loc,
    z_send, z_recv, zb_send, zb_recv, a_send, a_recv, b_send, b_recv,
    f_send, f_recv, fb_send, fb_recv, r_send, r_recv, l_send, l_recv,
    g_send, g_recv, c_send, c_recv, d_send, d_recv, s_send, s_recv, t_send, t_recv,
):
    me = lax.axis_index("expert")
    experts = layers * 8
    z, place = me // 8, me % 8
    y, x, core = place // 4, (place // 2) % 2, place % 2
    micro, part, width = x_hbm.shape
    picks = ids.shape[0]
    rows = micro * part
    many = 4 * rows
    half = rows // 2
    late = rows // 4
    early = rows - late

    def at(layer, row, column, side):
        return ((layer * 2 + row) * 2 + column) * 2 + side

    partner = at(z, y, x, 1 - core)
    peers = [at(z, y, 1 - x, core), at(z, 1 - y, x, core)]
    plane = peers + [at(z, 1 - y, 1 - x, core)]

    def in_column(layer):
        return at(layer, y, x, core)

    upper = z // (layers // 2)
    depth = z + upper * (layers - 1 - 2 * z)

    def layer_of(t):
        over = (t - 2 * depth - 1 + 4 * layers) // (4 * layers)
        odd = t % 2
        near = odd * (depth + (t + 1) // 2) + (1 - odd) * (depth - t // 2)
        found = over * t + (1 - over) * near
        return found + upper * (layers - 1 - 2 * found)

    def remote(src, dst, send, recv, device):
        return pltpu.make_async_remote_copy(
            src_ref=src, dst_ref=dst, send_sem=send, recv_sem=recv,
            device_id={"expert": device}, device_id_type=pl.DeviceIdType.MESH,
        )

    first_rows, last_rows = pl.ds(0, early), pl.ds(early, late)

    def weight_copy(i):
        return remote(
            (wg_hbm, wu_hbm, wd_hbm)[i], (wg, wu, wd)[i].at[1], w_send.at[i], w_recv.at[i], partner
        )

    def weight_local(i):
        return pltpu.make_async_copy(
            (wg_hbm, wu_hbm, wd_hbm)[i], (wg, wu, wd)[i].at[0], w_loc.at[i]
        )

    def column_gather(layer, way, source=None):
        to = in_column((z + 2 * way - 1 + layers) % layers)
        part_at = gathered.at[layer, 0, first_rows]
        return remote(
            part_at if source is None else source, part_at,
            z_send.at[layer, way], z_recv.at[layer], to,
        )

    def group_gather(layer, way):
        to = in_column((z + 2 * way - 1 + layers) % layers)
        part_at = gathered.at[layer, :, last_rows]
        return remote(part_at, part_at, zb_send.at[layer, way], zb_recv.at[layer], to)

    def plane_gather(layer, side, piece, own=False):
        mine = pl.ds((side + piece) % 2 * (early // 2), early // 2)
        return remote(
            xv.at[0, mine] if own else gathered.at[layer, 0, mine],
            gathered.at[layer, 1 + side, mine],
            a_send.at[layer, side, piece], a_recv.at[layer, side, piece], peers[side],
        )

    def start_plane(layer, own=False):
        for piece in range(2):
            for side in range(2):
                plane_gather(layer, side, piece, own).start()

    def start_forward(layer):
        for side in range(2):
            plane_gather(layer, side, 0).wait_recv()
            forward(layer, side).start()

    def plane_group(side):
        return remote(
            xv.at[0, last_rows], gathered.at[z, 1 + side, last_rows],
            b_send.at[side], b_recv.at[side], peers[side],
        )

    def forward(layer, side):
        mine = pl.ds(side * (early // 2), early // 2)
        return remote(
            gathered.at[layer, 1 + side, mine], gathered.at[layer, 3, mine],
            f_send.at[layer, side], f_recv.at[layer, side], peers[1 - side],
        )

    def forward_group(side):
        mine = pl.ds(early + side * (late // 2), late // 2)
        return remote(
            gathered.at[z, 1 + side, mine], gathered.at[z, 3, mine],
            fb_send.at[side], fb_recv.at[side], peers[1 - side],
        )

    def slot_of(t):
        if isinstance(t, int):
            return t if t < 2 else 2 + t % 2
        return 2 + t % 2

    def plane_reduce(t, k):
        return remote(
            staged.at[slot_of(t), 1 + k], plane_in.at[t, k],
            r_send.at[t, k], r_recv.at[t, k], peers[k],
        )

    def diag_reduce(t, side):
        return remote(
            staged.at[slot_of(t), 3, pl.ds(side * half, half)], diag_in.at[t, side],
            r_send.at[t, 2 + side], r_recv.at[t, 2 + side], peers[side],
        )

    def layer_reduce(t):
        return remote(
            layer_out.at[t], layer_in.at[z], l_send.at[t], l_recv.at[z], in_column(layer_of(t))
        )

    def layer_arrival(layer):
        return remote(
            layer_out.at[2], layer_in.at[layer], l_send.at[2], l_recv.at[layer], in_column(layer)
        )

    central = depth // (layers // 2 - 1)

    def group_reduce(kind):
        return remote(
            staged.at[1], group_in.at[kind], g_send.at[0], g_recv.at[kind],
            in_column(layer_of(1)),
        )

    def facts_column(to, source):
        return remote(
            facts.at[0, source], facts.at[0, source], c_send.at[to], c_recv.at[source],
            in_column(to),
        )

    def facts_plane(q):
        return remote(facts.at[0], facts.at[q], d_send.at[q], d_recv.at[q], plane[q - 1])

    def score_plane(t, q):
        return remote(
            score_out.at[t, q], score_in.at[t, q], s_send.at[t, q], s_recv.at[t, q],
            plane[q - 1],
        )

    def score_column(t):
        return remote(
            score_in.at[t], score_all.at[z], t_send.at[t], t_recv.at[z], in_column(layer_of(t))
        )

    def score_arrival(layer):
        return remote(
            score_in.at[1], score_all.at[layer], t_send.at[1], t_recv.at[layer],
            in_column(layer),
        )

    def start_scores(t):
        for q in range(1, 4):
            score_plane(t, q).start()

    def pass_scores(t):
        score_in[t, 0] = score_out[t, 0]
        for q in range(1, 4):
            score_plane(t, q).wait_recv()

    def passes(layer, way):
        if way == 1:
            return jnp.logical_and(layer < z, z < layers - 1)
        return jnp.logical_and(layer > z, z > 0)

    def relayed(layer):
        return jnp.logical_or(passes(layer, 0), passes(layer, 1))

    def relay(copy, layer):
        @pl.when(relayed(layer))
        def _():
            copy(layer, 0).wait_recv()
            for way in range(2):
                @pl.when(passes(layer, way))
                def _():
                    copy(layer, way).start()

    def arrive(copy, layer):
        @pl.when(jnp.logical_not(relayed(layer)))
        def _():
            copy(layer, 0).wait_recv()

    def both_ways(act):
        @pl.when(z < layers - 1)
        def _():
            act(1)

        @pl.when(z > 0)
        def _():
            act(0)

    barrier = pltpu.get_barrier_semaphore()
    greeted = [partner] + plane + [in_column((z + s) % layers) for s in range(1, layers)]
    for device in greeted:
        pl.semaphore_signal(
            barrier, inc=1, device_id={"expert": device}, device_id_type=pl.DeviceIdType.MESH
        )
    own = xv.at[0]
    local = [
        pltpu.make_async_copy(ids_hbm, ids, loc.at[0]),
        pltpu.make_async_copy(gates_hbm, gates, loc.at[1]),
    ]
    for m in range(micro):
        for i, source in enumerate((x_hbm, g_hbm)):
            local.append(
                pltpu.make_async_copy(
                    source.at[m], own.at[pl.ds(m * part, part), pl.ds(i * width, width)],
                    loc.at[2 + 2 * m + i],
                )
            )
    for copy in local:
        copy.start()
    for i in range(3):
        weight_local(i).start()
    for copy in local[:2]:
        copy.wait()

    def pick_row(k):
        return [
            jnp.concatenate([ref[k, m : m + 1, :] for m in range(micro)], axis=1)
            for ref in (ids, gates)
        ]

    facts[0, z] = jnp.where(
        lax.broadcasted_iota(jnp.int32, (16, rows), 0) < 8, 0.0, -1.0
    )
    for k in range(picks):
        names, values = pick_row(k)
        facts[0, z, k : k + 1, :] = values
        facts[0, z, 8 + k : 9 + k, :] = names.astype(jnp.float32)
    for copy in local[2:]:
        copy.wait()
    keep = pltpu.make_async_copy(
        own.at[last_rows], gathered.at[z, 0, last_rows], loc.at[0]
    )
    keep.start()
    pl.semaphore_wait(barrier, len(greeted))

    mine = xv.at[0, first_rows]
    for step in range(1, layers):
        facts_column((z + step) % layers, z).start()
    both_ways(lambda way: column_gather(z, way, mine).start())
    for side in range(2):
        plane_group(side).start()
    start_plane(z, True)
    for i in range(3):
        weight_copy(i).start()
    for side in range(2):
        plane_group(side).wait_recv()
        forward_group(side).start()
    start_forward(z)
    for step in range(1, layers):
        facts_column(z, (z + step) % layers).wait_recv()
    for q in range(1, 4):
        facts_plane(q).start()
    relay(column_gather, layer_of(1))
    relay(column_gather, layer_of(2))
    arrive(column_gather, layer_of(1))
    start_plane(layer_of(1))
    for side in range(2):
        forward_group(side).wait_recv()
    keep.wait()
    both_ways(lambda way: group_gather(z, way).start())
    relay(column_gather, layer_of(3))
    arrive(column_gather, layer_of(2))
    start_forward(layer_of(1))
    start_plane(layer_of(2))
    for i in range(3):
        weight_local(i).wait()
    for q in range(1, 4):
        facts_plane(q).wait_recv()

    lanes = lax.broadcasted_iota(jnp.int32, (rows, LANES), 1)

    def gates_of(layer, expert_id):
        chosen = []
        for q in range(4):
            values, names = facts[q, layer, 0:8, :], facts[q, layer, 8:16, :]
            named = jnp.where(names == expert_id.astype(jnp.float32), values, 0.0)
            chosen.append(jnp.sum(named, axis=0, keepdims=True))
        table = jnp.concatenate(chosen + chosen, axis=0).T
        return jnp.concatenate([table[:, q : q + 1] for q in range(4)], axis=0)

    def expert(j, expert_id, slot, t, layer, between=lambda: None):
        xs = xv[:, :, :width].reshape(many, width)
        gs = xv[:, :, width : 2 * width].reshape(many, width)
        gate_pre = jnp.dot(xs, wg[j], preferred_element_type=jnp.float32)
        up_pre = jnp.dot(xs, wu[j], preferred_element_type=jnp.float32)
        back = lax.dot_general(gs, wd[j], NT, preferred_element_type=jnp.float32)
        logistic = 1.0 / (1.0 + jnp.exp(-gate_pre))
        swish = gate_pre * logistic
        d_up = back * swish
        score = jnp.sum(d_up * up_pre, axis=1, keepdims=True)
        d_gate = (back * up_pre * logistic * (1.0 + gate_pre * (1.0 - logistic)))
        d_gate, d_up = d_gate.astype(jnp.bfloat16), d_up.astype(jnp.bfloat16)
        gate = gates_of(layer, expert_id)
        marked = jnp.zeros((rows, LANES), jnp.float32)
        for q in range(4):
            marked = marked + jnp.where(lanes == 8 * q + j, score[q * rows : (q + 1) * rows], 0.0)
        if j == 0:
            spread[...] = marked
        else:
            table = (spread[...] + marked).T
            for q in range(4):
                score_out[t, q] = table[8 * q : 8 * q + 8]
        between()
        tile = min(512, width)
        for col in range(0, width, tile):
            cols = pl.ds(col, tile)
            pair = lax.dot_general(d_gate, wg[j, cols, :], NT, preferred_element_type=jnp.float32)
            pair = pair + lax.dot_general(
                d_up, wu[j, cols, :], NT, preferred_element_type=jnp.float32
            )
            pair = gate * pair.astype(jnp.bfloat16).astype(jnp.float32)
            if j == 0:
                acc[:, cols] = pair
            else:
                staged[slot, :, :, cols] = (
                    (acc[:, cols] + pair).astype(jnp.bfloat16).reshape(4, rows, tile)
                )

    def start_diag(t):
        for side in range(2):
            diag_reduce(t, side).start()

    def merge_plane(t):
        for side in range(2):
            diag_reduce(t, side).wait_send()
            diag_reduce(t, side).wait_recv()
            mine = pl.ds(side * half, half)
            merged = staged[slot_of(t), 2 - side, mine].astype(jnp.float32)
            merged = merged + diag_in[t, side].astype(jnp.float32)
            staged[slot_of(t), 2 - side, mine] = merged.astype(jnp.bfloat16)
            plane_reduce(t, 1 - side).start()

    def plane_total(t):
        for k in range(2):
            plane_reduce(t, k).wait_send()
            plane_reduce(t, k).wait_recv()
        total = staged[slot_of(t), 0].astype(jnp.float32)
        for k in range(2):
            total = total + plane_in[t, k].astype(jnp.float32)
        return total

    def finish_plane(t):
        layer_out[t] = plane_total(t).astype(jnp.bfloat16)
        layer_reduce(t).start()

    def one_step(t, carry):
        layer = layer_of(t)
        following = layer_of(t + 1)

        @pl.when(t > 0)
        def _():
            arrive(group_gather, layer)

        for side in range(2):
            plane_gather(layer, side, 1).wait_recv()
            forward(layer, side).wait_recv()
        others = pltpu.make_async_copy(
            gathered.at[layer, pl.ds(1, 3)], xv.at[pl.ds(1, 3)], loc.at[1]
        )
        others.start()

        @pl.when(t > 0)
        def _():
            first = pltpu.make_async_copy(gathered.at[layer, 0], own, loc.at[2])
            first.start()
            first.wait()

        others.wait()
        def sums():
            @pl.when(t == 1)
            def _():
                pass_scores(0)
                score_all[z] = score_in[0]

            @pl.when(t > 1)
            def _():
                pass_scores(t - 1)
                score_column(t - 1).start()

            @pl.when(t > 3)
            def _():
                finish_plane(t - 2)

            @pl.when(t > 2)
            def _():
                merge_plane(t - 1)

        expert(0, me, 0, t, layer, sums)

        @pl.when(t == 0)
        def _():
            relay(group_gather, layer_of(1))

        @pl.when(t + 2 < layers)
        def _():
            relay(group_gather, layer_of(t + 2))

        @pl.when(t == 0)
        def _():
            for i in range(3):
                weight_copy(i).wait_recv()
            both_ways(lambda way: column_gather(z, way, mine).wait_send())
            for side in range(2):
                plane_group(side).wait_send()
                for piece in range(2):
                    plane_gather(z, side, piece, True).wait_send()

        later = (t + layers - 2) // layers
        slot = later * (2 + t % 2) + (1 - later) * t
        expert(1, partner, slot, t, layer)
        start_scores(t)

        @pl.when(t == 1)
        def _():
            group_reduce(central).start()

        @pl.when(t > 1)
        def _():
            start_diag(t)

        @pl.when(t + 2 < layers)
        def _():
            start_forward(layer_of(t + 2))

        @pl.when(t + 4 < layers)
        def _():
            relay(column_gather, layer_of(t + 4))

        @pl.when(t + 3 < layers)
        def _():
            arrive(column_gather, layer_of(t + 3))
            start_plane(layer_of(t + 3))

        return carry

    lax.fori_loop(0, layers, one_step, 0)
    finish_plane(layers - 2)
    pass_scores(layers - 1)
    score_column(layers - 1).start()
    merge_plane(layers - 1)
    for kind, there in enumerate((depth > 0, central > 0)):
        @pl.when(there)
        def _():
            group_reduce(kind).wait_recv()
            load = pltpu.make_async_copy(
                group_in.at[kind], xv.at[:, :, pl.ds(0, width)], loc.at[0]
            )
            load.start()
            load.wait()
            for i in range(4):
                merged = staged[0, i].astype(jnp.float32)
                merged = merged + xv[i, :, : width].astype(jnp.float32)
                staged[0, i] = merged.astype(jnp.bfloat16)

    start_diag(0)
    finish_plane(layers - 1)
    merge_plane(0)
    grads = [
        pltpu.make_async_copy(g_hbm.at[m], out_ref.at[m], loc.at[m]) for m in range(micro)
    ]
    for copy in grads:
        copy.start()
    acc[pl.ds(0, rows), :] = jnp.zeros((rows, width), jnp.float32)

    def add_layer(s, carry):
        layer = layer_of(s)

        @pl.when(jnp.logical_or(s > 2, jnp.where(s == 1, central, depth) == 0))
        def _():
            layer_arrival(layer).wait_recv()
            landed = xv.at[0, :, pl.ds(0, width)]
            load = pltpu.make_async_copy(layer_in.at[layer], landed, loc.at[micro])
            load.start()
            load.wait()
            acc[pl.ds(0, rows), :] += landed[...].astype(jnp.float32)

        return carry

    lax.fori_loop(1, layers, add_layer, 0)
    total = acc[pl.ds(0, rows), :] + plane_total(0)
    for m in range(micro):
        grads[m].wait()
        some = total[m * part : (m + 1) * part]
        out_ref[m] = (out_ref[m].astype(jnp.float32) + some).astype(jnp.bfloat16)
    for step in range(1, layers):
        score_arrival((z + step) % layers).wait_recv()
    count = layers * 4 * 8
    scores = score_all[...].reshape(count, rows).astype(jnp.bfloat16).astype(jnp.float32)
    entry = lax.broadcasted_iota(jnp.int32, (count, rows), 0)
    there, kind, which = entry // 32, (entry // 8) % 4, entry % 8
    owner = at(there, (y + kind // 2) % 2, (x + kind % 2) % 2, (core + which) % 2)
    owner = jnp.where(which < 2, owner, -1)
    for k in range(picks):
        names, _ = pick_row(k)
        chosen = jnp.sum(jnp.where(owner == names, scores, 0.0), axis=0, keepdims=True)
        for m in range(micro):
            score_ref[k, m : m + 1, :] = chosen[:, m * part : (m + 1) * part]

    for i in range(3):
        weight_copy(i).wait_send()
    for side in range(2):
        forward_group(side).wait_send()
        forward(z, side).wait_send()
    both_ways(lambda way: group_gather(z, way).wait_send())
    group_reduce(central).wait_send()
    for step in range(1, layers):
        facts_column((z + step) % layers, z).wait_send()
    for q in range(1, 4):
        facts_plane(q).wait_send()
        score_plane(0, q).wait_send()

    def settle(s, carry):
        layer = layer_of(s)
        score_column(s).wait_send()
        for q in range(1, 4):
            score_plane(s, q).wait_send()
        for side in range(2):
            for piece in range(2):
                plane_gather(layer, side, piece).wait_send()
            forward(layer, side).wait_send()

        @pl.when(s > 1)
        def _():
            layer_reduce(s).wait_send()

        for copy in (column_gather, group_gather):
            for way in range(2):
                @pl.when(passes(layer, way))
                def _():
                    copy(layer, way).wait_send()

        return carry

    lax.fori_loop(1, layers, settle, 0)


def section(inputs, grads, ids, gates, w_gate, w_up, w_down, experts):
    layers = experts // 8
    micro, part, width = inputs.shape
    picks = ids.shape[0]
    rows = micro * part
    hidden = w_gate.shape[1]
    wide, back = 2 * width, width
    bf16 = jnp.bfloat16
    sem = pltpu.SemaphoreType.DMA
    anywhere = pl.BlockSpec(memory_space=pl.ANY)
    vmem = pl.BlockSpec(memory_space=pltpu.VMEM)
    out, score, *_ = pl.pallas_call(
        functools.partial(section_kernel, layers),
        in_specs=[anywhere] * 7,
        out_specs=[vmem, vmem] + [anywhere] * 3,
        out_shape=[
            jax.ShapeDtypeStruct((micro, part, width), bf16),
            jax.ShapeDtypeStruct((picks, micro, part), jnp.float32),
            jax.ShapeDtypeStruct((layers, 4, rows, wide), bf16),
            jax.ShapeDtypeStruct((layers, rows, back), bf16),
            jax.ShapeDtypeStruct((2, 4, rows, back), bf16),
        ],
        scratch_shapes=[
            pltpu.VMEM((2, width, hidden), bf16),
            pltpu.VMEM((2, width, hidden), bf16),
            pltpu.VMEM((2, hidden, width), bf16),
            pltpu.VMEM((4, rows, wide), bf16),
            pltpu.VMEM((4 * rows, back), jnp.float32),
            pltpu.VMEM((4, 4, rows, back), bf16),
            pltpu.VMEM((layers, 2, rows, back), bf16),
            pltpu.VMEM((layers, 2, rows // 2, back), bf16),
            pltpu.VMEM((layers, rows, back), bf16),
            pltpu.VMEM((picks, micro, part), jnp.int32),
            pltpu.VMEM((picks, micro, part), jnp.float32),
            pltpu.VMEM((4, layers, 16, rows), jnp.float32),
            pltpu.VMEM((rows, LANES), jnp.float32),
            pltpu.VMEM((layers, 4, 8, rows), jnp.float32),
            pltpu.VMEM((layers, 4, 8, rows), jnp.float32),
            pltpu.VMEM((layers, 4, 8, rows), jnp.float32),
            sem((3,)), sem((3,)), sem((3,)), sem((2 + 2 * micro,)),
            sem((layers, 2)), sem((layers,)), sem((layers, 2)), sem((layers,)),
            sem((layers, 2, 2)), sem((layers, 2, 2)), sem((2,)), sem((2,)),
            sem((layers, 2)), sem((layers, 2)), sem((2,)), sem((2,)),
            sem((layers, 4)), sem((layers, 4)),
            sem((layers,)), sem((layers,)), sem((1,)), sem((2,)),
            sem((layers,)), sem((layers,)), sem((4,)), sem((4,)),
            sem((layers, 4)), sem((layers, 4)), sem((layers,)), sem((layers,)),
        ],
        compiler_params=pltpu.CompilerParams(
            collective_id=0, has_side_effects=True, vmem_limit_bytes=63 * 1024 * 1024
        ),
    )(inputs, grads, ids, gates, w_gate, w_up, w_down)
    return out, score


def on_device(inputs, grads_out, expert_ids, gate_values, w_gate, w_up, w_down):
    out, score = section(
        inputs[0], grads_out[0],
        jnp.transpose(expert_ids[0], (2, 0, 1)), jnp.transpose(gate_values[0], (2, 0, 1)),
        w_gate[0, 0], w_up[0, 0], w_down[0, 0], lax.axis_size("expert"),
    )
    received, gate_grad = out[None], jnp.transpose(score, (1, 2, 0))[None]
    sections = lax.axis_size("pipe")
    if sections > 1:
        received = lax.ppermute(
            received, "pipe", [(s, (s - 1) % sections) for s in range(sections)]
        )
    return (received, gate_grad)


def solution(mesh):
    tokens = P("pipe", None, "expert", None)
    weights = P("pipe", "expert", None, None)
    return jax.shard_map(
        on_device,
        mesh=mesh,
        in_specs=(tokens,) * 4 + (weights,) * 3,
        out_specs=(tokens, tokens),
        check_vma=False,
    )
```

```python
import functools

import jax
import jax.numpy as jnp
from jax import lax
from jax.experimental import pallas as pl
from jax.experimental.pallas import tpu as pltpu
from jax.sharding import PartitionSpec as P

LANES = 128
NT = (((1,), (1,)), ((), ()))


def section_kernel(
    layers, x_hbm, g_hbm, ids_hbm, gates_hbm, wg_hbm, wu_hbm, wd_hbm,
    out_ref, score_ref, gathered, layer_in, group_in,
    wg, wu, wd, xv, acc, staged, plane_in, diag_in, layer_out, ids, gates,
    facts, spread, score_out, score_in, score_all,
    w_loc, w_send, w_recv, loc,
    z_send, z_recv, zb_send, zb_recv, a_send, a_recv, b_send, b_recv,
    f_send, f_recv, fb_send, fb_recv, r_send, r_recv, l_send, l_recv,
    g_send, g_recv, c_send, c_recv, d_send, d_recv, s_send, s_recv, t_send, t_recv,
    q_send, q_recv, e_send, e_recv,
):
    me = lax.axis_index("expert")
    experts = layers * 8
    z, place = me // 8, me % 8
    y, x, core = place // 4, (place // 2) % 2, place % 2
    micro, part, width = x_hbm.shape
    picks = ids.shape[0]
    rows = micro * part
    many = 4 * rows
    half = rows // 2
    late = rows // 4
    early = rows - late

    def at(layer, row, column, side):
        return ((layer * 2 + row) * 2 + column) * 2 + side

    partner = at(z, y, x, 1 - core)
    peers = [at(z, y, 1 - x, core), at(z, 1 - y, x, core)]
    plane = peers + [at(z, 1 - y, 1 - x, core)]

    def in_column(layer):
        return at(layer, y, x, core)

    upper = z // (layers // 2)
    depth = z + upper * (layers - 1 - 2 * z)

    def layer_of(t):
        over = (t - 2 * depth - 1 + 4 * layers) // (4 * layers)
        odd = t % 2
        near = odd * (depth + (t + 1) // 2) + (1 - odd) * (depth - t // 2)
        found = over * t + (1 - over) * near
        return found + upper * (layers - 1 - 2 * found)

    def remote(src, dst, send, recv, device):
        return pltpu.make_async_remote_copy(
            src_ref=src, dst_ref=dst, send_sem=send, recv_sem=recv,
            device_id={"expert": device}, device_id_type=pl.DeviceIdType.MESH,
        )

    first_rows, last_rows = pl.ds(0, early), pl.ds(early, late)

    def weight_copy(i):
        return remote(
            (wg_hbm, wu_hbm, wd_hbm)[i], (wg, wu, wd)[i].at[1], w_send.at[i], w_recv.at[i], partner
        )

    def weight_local(i):
        return pltpu.make_async_copy(
            (wg_hbm, wu_hbm, wd_hbm)[i], (wg, wu, wd)[i].at[0], w_loc.at[i]
        )

    def column_gather(layer, way, source=None):
        to = in_column((z + 2 * way - 1 + layers) % layers)
        part_at = gathered.at[layer, 0, first_rows]
        return remote(
            part_at if source is None else source, part_at,
            z_send.at[layer, way], z_recv.at[layer], to,
        )

    def group_gather(layer, way):
        to = in_column((z + 2 * way - 1 + layers) % layers)
        part_at = gathered.at[layer, :, last_rows]
        return remote(part_at, part_at, zb_send.at[layer, way], zb_recv.at[layer], to)

    def plane_gather(layer, side, piece, own=False):
        mine = pl.ds((side + piece) % 2 * (early // 2), early // 2)
        return remote(
            xv.at[0, mine] if own else gathered.at[layer, 0, mine],
            gathered.at[layer, 1 + side, mine],
            a_send.at[layer, side, piece], a_recv.at[layer, side, piece], peers[side],
        )

    def start_plane(layer, own=False):
        for piece in range(2):
            for side in range(2):
                plane_gather(layer, side, piece, own).start()

    def start_forward(layer):
        for side in range(2):
            plane_gather(layer, side, 0).wait_recv()
            forward(layer, side).start()

    def plane_group(side):
        return remote(
            xv.at[0, last_rows], gathered.at[z, 1 + side, last_rows],
            b_send.at[side], b_recv.at[side], peers[side],
        )

    def forward(layer, side):
        mine = pl.ds(side * (early // 2), early // 2)
        return remote(
            gathered.at[layer, 1 + side, mine], gathered.at[layer, 3, mine],
            f_send.at[layer, side], f_recv.at[layer, side], peers[1 - side],
        )

    def forward_group(side):
        mine = pl.ds(early + side * (late // 2), late // 2)
        return remote(
            gathered.at[z, 1 + side, mine], gathered.at[z, 3, mine],
            fb_send.at[side], fb_recv.at[side], peers[1 - side],
        )

    def slot_of(t):
        if isinstance(t, int):
            return t if t < 2 else 2 + t % 2
        return 2 + t % 2

    def plane_reduce(t, k):
        return remote(
            staged.at[slot_of(t), 1 + k], plane_in.at[t, k],
            r_send.at[t, k], r_recv.at[t, k], peers[k],
        )

    def diag_reduce(t, side):
        return remote(
            staged.at[slot_of(t), 3, pl.ds(side * half, half)], diag_in.at[t, side],
            r_send.at[t, 2 + side], r_recv.at[t, 2 + side], peers[side],
        )

    def layer_reduce(t):
        return remote(
            layer_out.at[t], layer_in.at[z], l_send.at[t], l_recv.at[z], in_column(layer_of(t))
        )

    end = layers - 1
    tile = min(512, width)
    tiles = width // tile

    def plane_piece(i, k):
        cols = pl.ds(i * tile, tile)
        return remote(
            staged.at[slot_of(end), 1 + k, :, cols], plane_in.at[end, k, :, cols],
            q_send.at[i, k], q_recv.at[i, k], peers[k],
        )

    def diag_piece(i, side):
        cols = pl.ds(i * tile, tile)
        return remote(
            staged.at[slot_of(end), 3, pl.ds(side * half, half), cols],
            diag_in.at[end, side, :, cols],
            q_send.at[i, 2 + side], q_recv.at[i, 2 + side], peers[side],
        )

    def layer_piece(i, source, to):
        cols = pl.ds(i * tile, tile)
        return remote(
            layer_out.at[end, :, cols], layer_in.at[source, :, cols],
            e_send.at[i], e_recv.at[source, i], in_column(to),
        )

    def layer_arrival(layer):
        return remote(
            layer_out.at[2], layer_in.at[layer], l_send.at[2], l_recv.at[layer], in_column(layer)
        )

    central = depth // (layers // 2 - 1)

    def group_reduce(kind):
        return remote(
            staged.at[1], group_in.at[kind], g_send.at[0], g_recv.at[kind],
            in_column(layer_of(1)),
        )

    def facts_column(to, source):
        return remote(
            facts.at[0, source], facts.at[0, source], c_send.at[to], c_recv.at[source],
            in_column(to),
        )

    def facts_plane(q):
        return remote(facts.at[0], facts.at[q], d_send.at[q], d_recv.at[q], plane[q - 1])

    def score_plane(t, q):
        return remote(
            score_out.at[t, q], score_in.at[t, q], s_send.at[t, q], s_recv.at[t, q],
            plane[q - 1],
        )

    def score_column(t):
        return remote(
            score_in.at[t], score_all.at[z], t_send.at[t], t_recv.at[z], in_column(layer_of(t))
        )

    def score_arrival(layer):
        return remote(
            score_in.at[1], score_all.at[layer], t_send.at[1], t_recv.at[layer],
            in_column(layer),
        )

    def start_scores(t):
        for q in range(1, 4):
            score_plane(t, q).start()

    def pass_scores(t):
        score_in[t, 0] = score_out[t, 0]
        for q in range(1, 4):
            score_plane(t, q).wait_recv()

    def passes(layer, way):
        if way == 1:
            return jnp.logical_and(layer < z, z < layers - 1)
        return jnp.logical_and(layer > z, z > 0)

    def relayed(layer):
        return jnp.logical_or(passes(layer, 0), passes(layer, 1))

    def relay(copy, layer):
        @pl.when(relayed(layer))
        def _():
            copy(layer, 0).wait_recv()
            for way in range(2):
                @pl.when(passes(layer, way))
                def _():
                    copy(layer, way).start()

    def arrive(copy, layer):
        @pl.when(jnp.logical_not(relayed(layer)))
        def _():
            copy(layer, 0).wait_recv()

    def both_ways(act):
        @pl.when(z < layers - 1)
        def _():
            act(1)

        @pl.when(z > 0)
        def _():
            act(0)

    barrier = pltpu.get_barrier_semaphore()
    greeted = [partner] + plane + [in_column((z + s) % layers) for s in range(1, layers)]
    for device in greeted:
        pl.semaphore_signal(
            barrier, inc=1, device_id={"expert": device}, device_id_type=pl.DeviceIdType.MESH
        )
    own = xv.at[0]
    local = [
        pltpu.make_async_copy(ids_hbm, ids, loc.at[0]),
        pltpu.make_async_copy(gates_hbm, gates, loc.at[1]),
    ]
    for m in range(micro):
        for i, source in enumerate((x_hbm, g_hbm)):
            local.append(
                pltpu.make_async_copy(
                    source.at[m], own.at[pl.ds(m * part, part), pl.ds(i * width, width)],
                    loc.at[2 + 2 * m + i],
                )
            )
    for copy in local:
        copy.start()
    for i in range(3):
        weight_local(i).start()
    for copy in local[:2]:
        copy.wait()

    def pick_row(k):
        return [
            jnp.concatenate([ref[k, m : m + 1, :] for m in range(micro)], axis=1)
            for ref in (ids, gates)
        ]

    facts[0, z] = jnp.where(
        lax.broadcasted_iota(jnp.int32, (16, rows), 0) < 8, 0.0, -1.0
    )
    for k in range(picks):
        names, values = pick_row(k)
        facts[0, z, k : k + 1, :] = values
        facts[0, z, 8 + k : 9 + k, :] = names.astype(jnp.float32)
    for copy in local[2:]:
        copy.wait()
    keep = pltpu.make_async_copy(
        own.at[last_rows], gathered.at[z, 0, last_rows], loc.at[0]
    )
    keep.start()
    pl.semaphore_wait(barrier, len(greeted))

    mine = xv.at[0, first_rows]
    for step in range(1, layers):
        facts_column((z + step) % layers, z).start()
    both_ways(lambda way: column_gather(z, way, mine).start())
    for side in range(2):
        plane_group(side).start()
    start_plane(z, True)
    for i in range(3):
        weight_copy(i).start()
    for side in range(2):
        plane_group(side).wait_recv()
        forward_group(side).start()
    start_forward(z)
    for step in range(1, layers):
        facts_column(z, (z + step) % layers).wait_recv()
    for q in range(1, 4):
        facts_plane(q).start()
    relay(column_gather, layer_of(1))
    relay(column_gather, layer_of(2))
    arrive(column_gather, layer_of(1))
    start_plane(layer_of(1))
    for side in range(2):
        forward_group(side).wait_recv()
    keep.wait()
    both_ways(lambda way: group_gather(z, way).start())
    relay(column_gather, layer_of(3))
    arrive(column_gather, layer_of(2))
    start_forward(layer_of(1))
    start_plane(layer_of(2))
    for i in range(3):
        weight_local(i).wait()
    for q in range(1, 4):
        facts_plane(q).wait_recv()

    lanes = lax.broadcasted_iota(jnp.int32, (rows, LANES), 1)

    def gates_of(layer, expert_id):
        chosen = []
        for q in range(4):
            values, names = facts[q, layer, 0:8, :], facts[q, layer, 8:16, :]
            named = jnp.where(names == expert_id.astype(jnp.float32), values, 0.0)
            chosen.append(jnp.sum(named, axis=0, keepdims=True))
        table = jnp.concatenate(chosen + chosen, axis=0).T
        return jnp.concatenate([table[:, q : q + 1] for q in range(4)], axis=0)

    def expert(j, expert_id, slot, t, layer, between=lambda: None, ready=lambda: None):
        xs = xv[:, :, :width].reshape(many, width)
        gate_pre = jnp.dot(xs, wg[j], preferred_element_type=jnp.float32)
        up_pre = jnp.dot(xs, wu[j], preferred_element_type=jnp.float32)
        ready()
        gs = xv[:, :, width : 2 * width].reshape(many, width)
        back = lax.dot_general(gs, wd[j], NT, preferred_element_type=jnp.float32)
        logistic = 1.0 / (1.0 + jnp.exp(-gate_pre))
        swish = gate_pre * logistic
        d_up = back * swish
        score = jnp.sum(d_up * up_pre, axis=1, keepdims=True)
        d_gate = (back * up_pre * logistic * (1.0 + gate_pre * (1.0 - logistic)))
        d_gate, d_up = d_gate.astype(jnp.bfloat16), d_up.astype(jnp.bfloat16)
        gate = gates_of(layer, expert_id)
        marked = jnp.zeros((rows, LANES), jnp.float32)
        for q in range(4):
            marked = marked + jnp.where(lanes == 8 * q + j, score[q * rows : (q + 1) * rows], 0.0)
        if j == 0:
            spread[...] = marked
        else:
            table = (spread[...] + marked).T
            for q in range(4):
                score_out[t, q] = table[8 * q : 8 * q + 8]
        between()
        for piece in range(tiles):
            cols = pl.ds(piece * tile, tile)
            pair = lax.dot_general(d_gate, wg[j, cols, :], NT, preferred_element_type=jnp.float32)
            pair = pair + lax.dot_general(
                d_up, wu[j, cols, :], NT, preferred_element_type=jnp.float32
            )
            pair = gate * pair.astype(jnp.bfloat16).astype(jnp.float32)
            if j == 0:
                acc[:, cols] = pair
            else:
                staged[slot, :, :, cols] = (
                    (acc[:, cols] + pair).astype(jnp.bfloat16).reshape(4, rows, tile)
                )

                @pl.when(t == end)
                def _():
                    for side in range(2):
                        diag_piece(piece, side).start()


    def start_diag(t):
        for side in range(2):
            diag_reduce(t, side).start()

    def merge_plane(t):
        for side in range(2):
            diag_reduce(t, side).wait_send()
            diag_reduce(t, side).wait_recv()
            mine = pl.ds(side * half, half)
            merged = staged[slot_of(t), 2 - side, mine].astype(jnp.float32)
            merged = merged + diag_in[t, side].astype(jnp.float32)
            staged[slot_of(t), 2 - side, mine] = merged.astype(jnp.bfloat16)
            plane_reduce(t, 1 - side).start()

    def plane_total(t):
        for k in range(2):
            plane_reduce(t, k).wait_send()
            plane_reduce(t, k).wait_recv()
        total = staged[slot_of(t), 0].astype(jnp.float32)
        for k in range(2):
            total = total + plane_in[t, k].astype(jnp.float32)
        return total

    def merge_piece(i):
        cols = pl.ds(i * tile, tile)
        for side in range(2):
            diag_piece(i, side).wait_send()
            diag_piece(i, side).wait_recv()
            mine = pl.ds(side * half, half)
            merged = staged[slot_of(end), 2 - side, mine, cols].astype(jnp.float32)
            merged = merged + diag_in[end, side, :, cols].astype(jnp.float32)
            staged[slot_of(end), 2 - side, mine, cols] = merged.astype(jnp.bfloat16)
            plane_piece(i, 1 - side).start()

    def finish_piece(i):
        cols = pl.ds(i * tile, tile)
        for k in range(2):
            plane_piece(i, k).wait_send()
            plane_piece(i, k).wait_recv()
        total = staged[slot_of(end), 0, :, cols].astype(jnp.float32)
        for k in range(2):
            total = total + plane_in[end, k, :, cols].astype(jnp.float32)
        layer_out[end, :, cols] = total.astype(jnp.bfloat16)
        layer_piece(i, z, layer_of(end)).start()

    def finish_plane(t):
        layer_out[t] = plane_total(t).astype(jnp.bfloat16)
        layer_reduce(t).start()

    def one_step(t, carry):
        layer = layer_of(t)
        following = layer_of(t + 1)

        @pl.when(t > 0)
        def _():
            arrive(group_gather, layer)

        for side in range(2):
            plane_gather(layer, side, 1).wait_recv()
            forward(layer, side).wait_recv()
        def load(kind, start):
            cols = pl.ds(kind * width, width)
            others = pltpu.make_async_copy(
                gathered.at[layer, pl.ds(1, 3), :, cols], xv.at[pl.ds(1, 3), :, cols],
                loc.at[kind],
            )
            first = pltpu.make_async_copy(
                gathered.at[layer, 0, :, cols], xv.at[0, :, cols], loc.at[2 + kind]
            )
            others.start() if start else others.wait()

            @pl.when(t > 0)
            def _():
                first.start() if start else first.wait()

        for kind in range(2):
            load(kind, True)
        load(0, False)

        def sums():
            @pl.when(t == 1)
            def _():
                pass_scores(0)
                score_all[z] = score_in[0]

            @pl.when(t > 1)
            def _():
                pass_scores(t - 1)
                score_column(t - 1).start()

            @pl.when(t > 2)
            def _():
                merge_plane(t - 1)

        expert(0, me, 0, t, layer, sums, lambda: load(1, False))

        @pl.when(t == 0)
        def _():
            relay(group_gather, layer_of(1))

        @pl.when(t + 2 < layers)
        def _():
            relay(group_gather, layer_of(t + 2))

        @pl.when(t == 0)
        def _():
            for i in range(3):
                weight_copy(i).wait_recv()
            both_ways(lambda way: column_gather(z, way, mine).wait_send())
            for side in range(2):
                plane_group(side).wait_send()
                for piece in range(2):
                    plane_gather(z, side, piece, True).wait_send()

        later = (t + layers - 2) // layers
        slot = later * (2 + t % 2) + (1 - later) * t
        expert(1, partner, slot, t, layer)

        @pl.when(t > 2)
        def _():
            finish_plane(t - 1)

        start_scores(t)

        @pl.when(t == 1)
        def _():
            group_reduce(central).start()

        @pl.when(jnp.logical_and(t > 1, t < end))
        def _():
            start_diag(t)

        @pl.when(t + 2 < layers)
        def _():
            start_forward(layer_of(t + 2))

        @pl.when(t + 4 < layers)
        def _():
            relay(column_gather, layer_of(t + 4))

        @pl.when(t + 3 < layers)
        def _():
            arrive(column_gather, layer_of(t + 3))
            start_plane(layer_of(t + 3))

        return carry

    lax.fori_loop(0, layers, one_step, 0)
    for i in range(tiles):
        merge_piece(i)
    pass_scores(end)
    score_column(end).start()
    for i in range(tiles - 1):
        finish_piece(i)
    for kind, there in enumerate((depth > 0, central > 0)):
        @pl.when(there)
        def _():
            group_reduce(kind).wait_recv()
            load = pltpu.make_async_copy(
                group_in.at[kind], xv.at[:, :, pl.ds(0, width)], loc.at[0]
            )
            load.start()
            load.wait()
            for i in range(4):
                merged = staged[0, i].astype(jnp.float32)
                merged = merged + xv[i, :, : width].astype(jnp.float32)
                staged[0, i] = merged.astype(jnp.bfloat16)

    start_diag(0)
    finish_piece(tiles - 1)
    merge_plane(0)
    grads = [
        pltpu.make_async_copy(g_hbm.at[m], out_ref.at[m], loc.at[m]) for m in range(micro)
    ]
    for copy in grads:
        copy.start()
    acc[pl.ds(0, rows), :] = jnp.zeros((rows, width), jnp.float32)

    def add_layer(s, carry):
        layer = layer_of(s)

        @pl.when(jnp.logical_or(s > 2, jnp.where(s == 1, central, depth) == 0))
        def _():
            pieces = jnp.logical_and(depth == 0, layer // (layers // 2) != upper)

            @pl.when(pieces)
            def _():
                for i in range(tiles):
                    layer_piece(i, layer, layer).wait_recv()

            @pl.when(jnp.logical_not(pieces))
            def _():
                layer_arrival(layer).wait_recv()

            landed = xv.at[0, :, pl.ds(0, width)]
            load = pltpu.make_async_copy(layer_in.at[layer], landed, loc.at[micro])
            load.start()
            load.wait()
            acc[pl.ds(0, rows), :] += landed[...].astype(jnp.float32)

        return carry

    lax.fori_loop(1, layers, add_layer, 0)
    total = acc[pl.ds(0, rows), :] + plane_total(0)
    for m in range(micro):
        grads[m].wait()
        some = total[m * part : (m + 1) * part]
        out_ref[m] = (out_ref[m].astype(jnp.float32) + some).astype(jnp.bfloat16)
    for step in range(1, layers):
        score_arrival((z + step) % layers).wait_recv()
    count = layers * 4 * 8
    scores = score_all[...].reshape(count, rows).astype(jnp.bfloat16).astype(jnp.float32)
    entry = lax.broadcasted_iota(jnp.int32, (count, rows), 0)
    there, kind, which = entry // 32, (entry // 8) % 4, entry % 8
    owner = at(there, (y + kind // 2) % 2, (x + kind % 2) % 2, (core + which) % 2)
    owner = jnp.where(which < 2, owner, -1)
    for k in range(picks):
        names, _ = pick_row(k)
        chosen = jnp.sum(jnp.where(owner == names, scores, 0.0), axis=0, keepdims=True)
        for m in range(micro):
            score_ref[k, m : m + 1, :] = chosen[:, m * part : (m + 1) * part]

    for i in range(3):
        weight_copy(i).wait_send()
    for side in range(2):
        forward_group(side).wait_send()
        forward(z, side).wait_send()
    both_ways(lambda way: group_gather(z, way).wait_send())
    group_reduce(central).wait_send()
    for i in range(tiles):
        layer_piece(i, z, layer_of(end)).wait_send()
    for step in range(1, layers):
        facts_column((z + step) % layers, z).wait_send()
    for q in range(1, 4):
        facts_plane(q).wait_send()
        score_plane(0, q).wait_send()

    def settle(s, carry):
        layer = layer_of(s)
        score_column(s).wait_send()
        for q in range(1, 4):
            score_plane(s, q).wait_send()
        for side in range(2):
            for piece in range(2):
                plane_gather(layer, side, piece).wait_send()
            forward(layer, side).wait_send()

        @pl.when(jnp.logical_and(s > 1, s < end))
        def _():
            layer_reduce(s).wait_send()

        for copy in (column_gather, group_gather):
            for way in range(2):
                @pl.when(passes(layer, way))
                def _():
                    copy(layer, way).wait_send()

        return carry

    lax.fori_loop(1, layers, settle, 0)


def section(inputs, grads, ids, gates, w_gate, w_up, w_down, experts):
    layers = experts // 8
    micro, part, width = inputs.shape
    picks = ids.shape[0]
    rows = micro * part
    tiles = width // min(512, width)
    hidden = w_gate.shape[1]
    wide, back = 2 * width, width
    bf16 = jnp.bfloat16
    sem = pltpu.SemaphoreType.DMA
    anywhere = pl.BlockSpec(memory_space=pl.ANY)
    vmem = pl.BlockSpec(memory_space=pltpu.VMEM)
    out, score, *_ = pl.pallas_call(
        functools.partial(section_kernel, layers),
        in_specs=[anywhere] * 7,
        out_specs=[vmem, vmem] + [anywhere] * 3,
        out_shape=[
            jax.ShapeDtypeStruct((micro, part, width), bf16),
            jax.ShapeDtypeStruct((picks, micro, part), jnp.float32),
            jax.ShapeDtypeStruct((layers, 4, rows, wide), bf16),
            jax.ShapeDtypeStruct((layers, rows, back), bf16),
            jax.ShapeDtypeStruct((2, 4, rows, back), bf16),
        ],
        scratch_shapes=[
            pltpu.VMEM((2, width, hidden), bf16),
            pltpu.VMEM((2, width, hidden), bf16),
            pltpu.VMEM((2, hidden, width), bf16),
            pltpu.VMEM((4, rows, wide), bf16),
            pltpu.VMEM((4 * rows, back), jnp.float32),
            pltpu.VMEM((4, 4, rows, back), bf16),
            pltpu.VMEM((layers, 2, rows, back), bf16),
            pltpu.VMEM((layers, 2, rows // 2, back), bf16),
            pltpu.VMEM((layers, rows, back), bf16),
            pltpu.VMEM((picks, micro, part), jnp.int32),
            pltpu.VMEM((picks, micro, part), jnp.float32),
            pltpu.VMEM((4, layers, 16, rows), jnp.float32),
            pltpu.VMEM((rows, LANES), jnp.float32),
            pltpu.VMEM((layers, 4, 8, rows), jnp.float32),
            pltpu.VMEM((layers, 4, 8, rows), jnp.float32),
            pltpu.VMEM((layers, 4, 8, rows), jnp.float32),
            sem((3,)), sem((3,)), sem((3,)), sem((2 + 2 * micro,)),
            sem((layers, 2)), sem((layers,)), sem((layers, 2)), sem((layers,)),
            sem((layers, 2, 2)), sem((layers, 2, 2)), sem((2,)), sem((2,)),
            sem((layers, 2)), sem((layers, 2)), sem((2,)), sem((2,)),
            sem((layers, 4)), sem((layers, 4)),
            sem((layers,)), sem((layers,)), sem((1,)), sem((2,)),
            sem((layers,)), sem((layers,)), sem((4,)), sem((4,)),
            sem((layers, 4)), sem((layers, 4)), sem((layers,)), sem((layers,)),
            sem((tiles, 4)), sem((tiles, 4)), sem((tiles,)), sem((layers, tiles)),
        ],
        compiler_params=pltpu.CompilerParams(
            collective_id=0, has_side_effects=True, vmem_limit_bytes=63 * 1024 * 1024
        ),
    )(inputs, grads, ids, gates, w_gate, w_up, w_down)
    return out, score


def on_device(inputs, grads_out, expert_ids, gate_values, w_gate, w_up, w_down):
    out, score = section(
        inputs[0], grads_out[0],
        jnp.transpose(expert_ids[0], (2, 0, 1)), jnp.transpose(gate_values[0], (2, 0, 1)),
        w_gate[0, 0], w_up[0, 0], w_down[0, 0], lax.axis_size("expert"),
    )
    received, gate_grad = out[None], jnp.transpose(score, (1, 2, 0))[None]
    sections = lax.axis_size("pipe")
    if sections > 1:
        received = lax.ppermute(
            received, "pipe", [(s, (s - 1) % sections) for s in range(sections)]
        )
    return (received, gate_grad)


def solution(mesh):
    tokens = P("pipe", None, "expert", None)
    weights = P("pipe", "expert", None, None)
    return jax.shard_map(
        on_device,
        mesh=mesh,
        in_specs=(tokens,) * 4 + (weights,) * 3,
        out_specs=(tokens, tokens),
        check_vma=False,
    )
```
